32 devices in a mesh: gx: 8 (over y, x, core), gy: 4 (over z).
Axes of the slice: x: 2, y: 2, z: 4, core: 2. Of those that a mesh axis runs over, the one named last changes fastest.
Arguments:
- tracer_amounts: bfloat16 [2, 512, 512, 128], P(None, ('gx', 'gy')), may hold values from 0.099609375 to 3
- zonal_transit_ratio: float32 [2, 512, 512], P(None, 'gx', 'gy'), may hold values from -0.5 to 0.5
- meridional_transit_ratio: float32 [2, 512, 512], P(None, 'gx', 'gy'), may hold values from -0.45 to 0.45
- moisture_ratio: float32 [2, 512, 512], P(None, 'gx', 'gy'), may hold values from 0.2 to 0.9
- stratum_depths: float32 [2, 512, 512], P(None, 'gx', 'gy'), may hold values from 0.5 to 2
- sun_elevation_factor: float32 [512, 512], P('gx', 'gy'), may hold values from 0.2 to 1
- thermal_anomaly: float32 [2, 512, 512], P(None, 'gx', 'gy'), may hold values from -6 to 6
- particle_class_map: int32 [512, 512], P(('gx', 'gy')), may hold values from 0 to 7
- ground_cover_kind: int32 [512, 512], P(('gx', 'gy')), may hold values from 0 to 23
- arid_extinction_table: bfloat16 [128, 64], replicated, may hold values from 0 to 0.015625
- swelling_factors: bfloat16 [128, 64], replicated, may hold values from 0 to 0.00390625
- settling_velocities: float32 [24, 128], replicated, may hold values from 0.05 to 2
- arriving_irradiance: float32 [4], replicated, may hold values from 0.5 to 2
Outputs:
- updated_tracer_amounts: float32 [2, 512, 512, 128], P(None, ('gx', 'gy'))
- updated_thermal_anomaly: float32 [2, 512, 512], P(None, 'gx', 'gy')
The draws below stay inside these ranges and needn't reach their ends.
All inputs are finite; a program needn't handle non-finite values.
Results may differ from the reference program's by a relative error of at most 0.00075.
Values may be sent and summed in bfloat16 or wider, within the bound.
A program may use at most 128 MiB of HBM per device.

```python
import math
import jax
import jax.numpy as jnp
from jax import lax

S = 128
VERTICAL_TIERS = 2
SUB = 3
NBIN = 8
NW = 4
NLU = 24
ZONAL_POINTS = 512
MERIDIONAL_NODES = 512


def touch_ends(drawn, own_key, least, largest):
    place = [jax.random.randint(jax.random.fold_in(own_key, axis), (), 0, length) for axis, length in enumerate(drawn.shape)]
    main_axis = drawn.shape.index(max(drawn.shape))
    neighbour = place[:main_axis] + [(place[main_axis] + 1) % drawn.shape[main_axis]] + place[main_axis + 1:]
    return drawn.at[tuple(place)].set(least).at[tuple(neighbour)].set(largest)


def shard_levels(own_key, dims, split, least, largest):
    level = 1.0
    for dim, parts in split:
        steps = jax.random.uniform(jax.random.fold_in(jax.random.fold_in(own_key, 6), dim), (parts,), jnp.float32, least / len(split), largest / len(split))
        level = level * jnp.repeat(jnp.exp(steps), dims[dim] // parts).reshape((-1,) + (1,) * (len(dims) - 1 - dim))
    return level


def centred(own_key, shape, scale, most, cuts=(), held_as=jnp.bfloat16):
    loudness = shard_levels(own_key, shape, cuts, -0.22, 0.18) if cuts else 1.0
    entries = jax.random.normal(own_key, shape, jnp.float32) * scale * loudness
    return jnp.minimum(jnp.maximum(entries, -most), most).astype(held_as)


def setup_inputs(seed: int = 0) -> dict:
    streams_of = jax.random.split(jax.random.key(seed), 14)
    return {
        "tracer_amounts": jnp.clip(jnp.exp(math.log(3.0) - 3.4051113 * jax.random.uniform(streams_of[0], (VERTICAL_TIERS, ZONAL_POINTS, MERIDIONAL_NODES, S), jnp.float32) ** shard_levels(streams_of[0], (VERTICAL_TIERS, ZONAL_POINTS, MERIDIONAL_NODES, S), ((1, 32),), -0.2, 0.2)), 0.099609375, 3.0).astype(jnp.bfloat16),
        "zonal_transit_ratio": jnp.clip(jax.random.uniform(streams_of[1], (VERTICAL_TIERS, ZONAL_POINTS, MERIDIONAL_NODES), jnp.float32, -0.5, 0.5) * shard_levels(streams_of[1], (VERTICAL_TIERS, ZONAL_POINTS, MERIDIONAL_NODES), ((1, 8), (2, 4)), -0.4, 0.0), -0.5, 0.5),
        "meridional_transit_ratio": jnp.clip(jax.random.uniform(streams_of[2], (VERTICAL_TIERS, ZONAL_POINTS, MERIDIONAL_NODES), jnp.float32, -0.45, 0.45) * shard_levels(streams_of[2], (VERTICAL_TIERS, ZONAL_POINTS, MERIDIONAL_NODES), ((1, 8), (2, 4)), -0.4, 0.0), -0.45, 0.45),
        "moisture_ratio": jnp.clip(0.2 + 0.7 * jax.random.uniform(streams_of[3], (VERTICAL_TIERS, ZONAL_POINTS, MERIDIONAL_NODES), jnp.float32) ** shard_levels(streams_of[3], (VERTICAL_TIERS, ZONAL_POINTS, MERIDIONAL_NODES), ((1, 8), (2, 4)), -0.2, 0.2), 0.2, 0.9),
        "stratum_depths": jnp.clip(jnp.exp(math.log(2.0) - 1.3862944 * jax.random.uniform(streams_of[4], (VERTICAL_TIERS, ZONAL_POINTS, MERIDIONAL_NODES), jnp.float32) ** shard_levels(streams_of[4], (VERTICAL_TIERS, ZONAL_POINTS, MERIDIONAL_NODES), ((1, 8), (2, 4)), -0.2, 0.2)), 0.5, 2.0),
        "sun_elevation_factor": jnp.clip(jnp.exp(math.log(1.0) - 1.609438 * jax.random.uniform(streams_of[5], (ZONAL_POINTS, MERIDIONAL_NODES), jnp.float32) ** shard_levels(streams_of[5], (ZONAL_POINTS, MERIDIONAL_NODES), ((0, 8), (1, 4)), -0.2, 0.2)), 0.2, 1.0),
        "thermal_anomaly": centred(streams_of[6], (VERTICAL_TIERS, ZONAL_POINTS, MERIDIONAL_NODES), 1.0, 6.0, ((1, 8), (2, 4)), jnp.float32),
        "particle_class_map": touch_ends(jax.random.randint(streams_of[7], (ZONAL_POINTS, MERIDIONAL_NODES), 0, NBIN), jax.random.fold_in(streams_of[7], 1), 0, NBIN - 1).astype(jnp.int32),
        "ground_cover_kind": touch_ends(jax.random.randint(streams_of[8], (ZONAL_POINTS, MERIDIONAL_NODES), 0, NLU), jax.random.fold_in(streams_of[8], 1), 0, NLU - 1).astype(jnp.int32),
        "arid_extinction_table": jnp.clip(jax.random.uniform(streams_of[9], (S, 2 * NBIN * NW), jnp.float32, 0.0, 0.015625), 0.0, 0.015625).astype(jnp.bfloat16),
        "swelling_factors": jnp.clip(jax.random.uniform(streams_of[10], (S, 2 * NBIN * NW), jnp.float32, 0.0, 0.00390625), 0.0, 0.00390625).astype(jnp.bfloat16),
        "settling_velocities": jnp.clip(jnp.exp(jax.random.uniform(streams_of[11], (NLU, S), jnp.float32, math.log(0.05), math.log(2.0))), 0.05, 2.0),
        "arriving_irradiance": jnp.clip(jnp.exp(jax.random.uniform(streams_of[12], (NW,), jnp.float32, math.log(0.5), math.log(2.0))), 0.5, 2.0),
    }


SPREAD_FACTOR = 0.2
group_width = 16


def upwind(tracer, west_side, east_side, south_side, north_side, east_courant, north_courant):
    return (tracer - jnp.maximum(east_courant, 0.0) * (tracer - west_side)
            - jnp.minimum(east_courant, 0.0) * (east_side - tracer)
            - jnp.maximum(north_courant, 0.0) * (tracer - south_side)
            - jnp.minimum(north_courant, 0.0) * (north_side - tracer))


def radiate(optical, cosine, sunlight):
    layers_count = optical.shape[0]
    wavelengths = optical.shape[1] // 2
    weights = sunlight.reshape((wavelengths,) + (1,) * (optical.ndim - 2))
    overhead = jnp.zeros_like(optical[0, :wavelengths])
    layers = [None] * layers_count
    for height in reversed(range(layers_count)):
        transmitted = jnp.exp(-overhead / cosine)
        layers[height] = cosine * jnp.sum(weights * optical[height, wavelengths:] * transmitted, axis=0)
        overhead = overhead + optical[height, :wavelengths]
    return jnp.stack(layers)


def reference(tracer_amounts, zonal_transit_ratio, meridional_transit_ratio, moisture_ratio, stratum_depths, sun_elevation_factor, thermal_anomaly,
              particle_class_map, ground_cover_kind, arid_extinction_table, swelling_factors, settling_velocities, arriving_irradiance):
    group_count = S // group_width
    columns_all = 4 * NBIN * NW
    half_cols = 2 * NBIN * NW
    table_all = jnp.concatenate([arid_extinction_table, swelling_factors], axis=1).reshape(group_count, group_width, columns_all)
    velocity = jnp.moveaxis(settling_velocities.reshape(NLU, group_count, group_width), 1, 0)
    bin_mask = (particle_class_map[..., None] == jnp.arange(NBIN, dtype=jnp.int32)).astype(jnp.float32)
    level_outs = []
    optical_levels = []
    for height in range(VERTICAL_TIERS):
        east_courant = zonal_transit_ratio[height][..., None]
        north_courant = meridional_transit_ratio[height][..., None]
        groups = jnp.moveaxis(tracer_amounts[height].reshape(ZONAL_POINTS, MERIDIONAL_NODES, group_count, group_width), 2, 0)

        def advance_group(accumulated, members, height=height, east_courant=east_courant,
                          north_courant=north_courant):
            species_block, velocity_rows, table_rows = members
            tracer = species_block.astype(jnp.float32)
            for substep in range(SUB):
                padded = jnp.pad(tracer, ((1, 1), (0, 0), (0, 0)))
                padded_y = jnp.pad(tracer, ((0, 0), (1, 1), (0, 0)))
                tracer = upwind(tracer, padded[:-2], padded[2:], padded_y[:, :-2], padded_y[:, 2:],
                                east_courant, north_courant)
            if height == 0:
                loss_rate = velocity_rows[ground_cover_kind] / stratum_depths[0][..., None]
                tracer = tracer / (1.0 + loss_rate)
            rounded = tracer.astype(jnp.bfloat16)
            accumulated = accumulated + jnp.dot(rounded.reshape(ZONAL_POINTS * MERIDIONAL_NODES, group_width), table_rows,
                                                preferred_element_type=jnp.float32)
            return accumulated, tracer

        products, tracers = lax.scan(advance_group, jnp.zeros((ZONAL_POINTS * MERIDIONAL_NODES, columns_all), jnp.float32),
                                     (groups, velocity, table_all))
        level_outs.append(jnp.moveaxis(tracers, 0, 2).reshape(ZONAL_POINTS, MERIDIONAL_NODES, S))
        dry = products[:, :half_cols].reshape(ZONAL_POINTS, MERIDIONAL_NODES, NBIN, 2 * NW)
        wet = products[:, half_cols:].reshape(ZONAL_POINTS, MERIDIONAL_NODES, NBIN, 2 * NW)
        growth = moisture_ratio[height] / (1.0 - moisture_ratio[height])
        combined = dry + growth[..., None, None] * wet
        selected = jnp.sum(combined * bin_mask[..., None], axis=2)
        optical_levels.append(jnp.moveaxis(selected * stratum_depths[height][..., None], 2, 0))
    updated_tracer_amounts = jnp.stack(level_outs)
    optical = jnp.stack(optical_levels)
    warming_tendency = radiate(optical, sun_elevation_factor, arriving_irradiance)
    framed_thermal_field = jnp.pad(thermal_anomaly, ((0, 0), (1, 1), (1, 1)))
    second_difference_map = (framed_thermal_field[:, 2:, 1:-1] + framed_thermal_field[:, :-2, 1:-1] + framed_thermal_field[:, 1:-1, 2:]
               + framed_thermal_field[:, 1:-1, :-2] - 4.0 * thermal_anomaly)
    updated_thermal_anomaly = thermal_anomaly + SPREAD_FACTOR * second_difference_map + warming_tendency
    return updated_tracer_amounts, updated_thermal_anomaly
```

```python
import functools

import jax
import jax.numpy as jnp
from jax import lax
from jax.experimental import pallas as pl
from jax.experimental.pallas import tpu as pltpu
from jax.sharding import PartitionSpec as P

SUB = 3
NBIN = 8
NW = 4
SPREAD_FACTOR = 0.2
PAD = 8
LAND_ROWS = 32
MESH = pl.DeviceIdType.MESH
VMEM_SPEC = pl.BlockSpec(memory_space=pltpu.VMEM)
SMEM_SPEC = pl.BlockSpec(memory_space=pltpu.SMEM)


def greet(gx_count, gy_count, reach):
    gx = lax.axis_index("gx")
    gy = lax.axis_index("gy")
    barrier = pltpu.get_barrier_semaphore()
    for dx in range(-reach, reach + 1):
        for dy in range(gy_count):
            if dx == 0 and dy == 0:
                continue
            pl.semaphore_signal(
                barrier,
                inc=1,
                device_id=(
                    lax.rem(gx + dx + gx_count, gx_count),
                    lax.rem(gy + dy, gy_count),
                ),
                device_id_type=MESH,
            )
    pl.semaphore_wait(barrier, (2 * reach + 1) * gy_count - 1)


def fields_kernel(
    gx_count, gy_count, width,
    fields, sun, fringe,
    strip, rim, strip_sun, fringe_in,
    send_a, recv_a, send_s, recv_s, send_r, recv_r, send_f, recv_f,
):
    gx = lax.axis_index("gx")
    gy = lax.axis_index("gy")
    span = width + 2 * SUB
    tile_x = width * gy_count
    tile_y = fields.shape[2]
    right = lax.rem(gx + 1, gx_count)
    left = lax.rem(gx + gx_count - 1, gx_count)
    up = lax.rem(gy + 1, gy_count)
    down = lax.rem(gy + gy_count - 1, gy_count)
    greet(gx_count, gy_count, 1)
    mine = pl.ds(pl.multiple_of(gy * tile_y, tile_y), tile_y)

    def rims(side):
        lo = tile_x if side == 0 else SUB
        return pltpu.make_async_remote_copy(
            src_ref=fields.at[pl.ds(lo, SUB)],
            dst_ref=rim.at[side, :, :, mine],
            send_sem=send_r.at[side],
            recv_sem=recv_r.at[gy],
            device_id=((right, 0) if side == 0 else (left, gy_count - 1)),
            device_id_type=MESH,
        )

    def slab(peer):
        return pltpu.make_async_remote_copy(
            src_ref=fields.at[pl.ds(peer * width, span)],
            dst_ref=strip.at[:, :, mine],
            send_sem=send_a.at[peer],
            recv_sem=recv_a.at[gy],
            device_id=(gx, peer),
            device_id_type=MESH,
        )

    def sunny(peer):
        return pltpu.make_async_remote_copy(
            src_ref=sun.at[pl.ds(peer * width, width)],
            dst_ref=strip_sun.at[:, mine],
            send_sem=send_s.at[peer],
            recv_sem=recv_s.at[gy],
            device_id=(gx, peer),
            device_id_type=MESH,
        )

    targets = ((left, gy), (right, gy), (gx, down), (gx, up))
    edges = [
        pltpu.make_async_remote_copy(
            src_ref=fringe.at[k],
            dst_ref=fringe_in.at[k],
            send_sem=send_f.at[k],
            recv_sem=recv_f.at[k],
            device_id=targets[k],
            device_id_type=MESH,
        )
        for k in range(4)
    ]
    for peer in range(gy_count):
        @pl.when(gy != peer)
        def _(peer=peer):
            slab(peer).start()
            sunny(peer).start()
    for side in range(2):
        rims(side).start()
    for edge in edges:
        edge.start()
    strip[:, :, mine] = fields[pl.ds(gy * width, span)]
    strip_sun[:, mine] = sun[pl.ds(pl.multiple_of(gy * width, width), width), :]
    for edge in edges:
        edge.wait()
    for side in range(2):
        rims(side).wait_send()
    for peer in range(gy_count):
        @pl.when(gy != peer)
        def _(peer=peer):
            slab(peer).wait_send()
            sunny(peer).wait_send()
            theirs = pl.ds(peer * tile_y, tile_y)
            pltpu.make_async_remote_copy(
                src_ref=fields.at[pl.ds(0, span)],
                dst_ref=strip.at[:, :, theirs],
                send_sem=send_a.at[peer],
                recv_sem=recv_a.at[peer],
                device_id=(gx, peer),
                device_id_type=MESH,
            ).wait_recv()
            pltpu.make_async_remote_copy(
                src_ref=sun.at[pl.ds(0, width)],
                dst_ref=strip_sun.at[:, theirs],
                send_sem=send_s.at[peer],
                recv_sem=recv_s.at[peer],
                device_id=(gx, peer),
                device_id_type=MESH,
            ).wait_recv()
    for side, owner, source in ((0, 0, left), (1, gy_count - 1, right)):
        @pl.when(gy == owner)
        def _(side=side, source=source):
            for peer in range(gy_count):
                pltpu.make_async_remote_copy(
                    src_ref=fields.at[pl.ds(0, SUB)],
                    dst_ref=rim.at[side, :, :, pl.ds(peer * tile_y, tile_y)],
                    send_sem=send_r.at[side],
                    recv_sem=recv_r.at[peer],
                    device_id=(source, peer),
                    device_id_type=MESH,
                ).wait_recv()


def return_kernel(
    gx_count, gy_count, width, heat, base, out, tile, send_sem, recv_sem
):
    gx = lax.axis_index("gx")
    gy = lax.axis_index("gy")
    tile_y = base.shape[2]
    greet(gx_count, gy_count, 0)

    def slab(peer):
        return pltpu.make_async_remote_copy(
            src_ref=heat.at[:, :, pl.ds(peer * tile_y, tile_y)],
            dst_ref=tile.at[pl.ds(gy * width, width)],
            send_sem=send_sem.at[peer],
            recv_sem=recv_sem.at[gy],
            device_id=(gx, peer),
            device_id_type=MESH,
        )

    for peer in range(gy_count):
        @pl.when(gy != peer)
        def _(peer=peer):
            slab(peer).start()
    mine = pl.ds(pl.multiple_of(gy * tile_y, tile_y), tile_y)
    tile[pl.ds(gy * width, width)] = heat[:, :, mine]
    for peer in range(gy_count):
        @pl.when(gy != peer)
        def _(peer=peer):
            slab(peer).wait_send()
            pltpu.make_async_remote_copy(
                src_ref=heat.at[:, :, pl.ds(0, tile_y)],
                dst_ref=tile.at[pl.ds(peer * width, width)],
                send_sem=send_sem.at[peer],
                recv_sem=recv_sem.at[peer],
                device_id=(gx, peer),
                device_id_type=MESH,
            ).wait_recv()
    for level in range(base.shape[0]):
        out[level] = base[level] + tile[:, level, :]


def tn_dot(left, right):
    return lax.dot_general(
        left, right, (((0,), (0,)), ((), ())), preferred_element_type=jnp.float32
    )


def three_parts(rows):
    high = rows.astype(jnp.bfloat16).astype(jnp.float32)
    rest = rows - high
    middle = rest.astype(jnp.bfloat16).astype(jnp.float32)
    return jnp.concatenate([high, middle, rest - middle], axis=0).astype(jnp.bfloat16)


def chem_kernel(levels, width, edge, *refs):
    if edge:
        (flags, rim, halo_w, halo_e, tracer, strip, sun, bins, kinds, table, settle, light,
         _out_in, _opt_in, out, opt, first, second, zonal, merid, rounded) = refs
    else:
        (tracer, strip, sun, bins, kinds, table, settle, light,
         out, opt, first, second, zonal, merid, rounded) = refs
    level = levels - 1 - pl.program_id(0)
    step = pl.program_id(1)
    ny = tracer.shape[2]
    fields = strip.shape[1]
    local = first.shape[0]
    chunk = 64

    def selector(row):
        which = lax.rem(lax.broadcasted_iota(jnp.int32, (3 * fields, 128), 0), fields)
        return jnp.where(which == row, 1.0, 0.0).astype(jnp.bfloat16)

    def coefficients(slot, rows):
        parts = three_parts(rows)
        zonal[slot] = tn_dot(parts, selector(level))
        merid[slot] = tn_dot(parts, selector(levels + level))

    def moved(source, slot, y):
        here = source[slot, pl.ds(PAD + y, chunk), :]
        c = zonal[slot, pl.ds(y, chunk), :]
        d = merid[slot, pl.ds(y, chunk), :]
        across = jnp.where(
            c > 0.0,
            source[slot - 1, pl.ds(PAD + y, chunk), :],
            source[slot + 1, pl.ds(PAD + y, chunk), :],
        )
        along = jnp.where(
            d > 0.0,
            source[slot, pl.ds(PAD - 1 + y, chunk), :],
            source[slot, pl.ds(PAD + 1 + y, chunk), :],
        )
        return here + jnp.abs(c) * (across - here) + jnp.abs(d) * (along - here)

    def advance(source, target, low, high):
        def column(slot, carry):
            for y in range(0, ny, chunk):
                target[slot, pl.ds(PAD + y, chunk), :] = moved(source, slot, y)
            return carry

        lax.fori_loop(low, high, column, 0)

    def prepare():
        advance(first, second, 1, local - 1)
        advance(second, first, 2, local - 2)

    @pl.when((pl.program_id(0) == 0) & (step == 0))
    def _():
        zeros = jnp.zeros((local, PAD, 128), jnp.float32)
        for buffer in (first, second):
            buffer[:, pl.ds(0, PAD), :] = zeros
            buffer[:, pl.ds(PAD + ny, PAD), :] = zeros

    body = pl.ds(PAD, ny)
    if edge:
        six = local - SUB

        @pl.when(step == 0)
        def _():
            for j in range(SUB):
                rows = jnp.where(flags[0] == 1, rim[0, j], strip[j])
                coefficients(j, jnp.where(flags[1] == 1, rows, 0.0))
                first[j, body, :] = halo_w[0, j].astype(jnp.float32)

            def load(j, carry):
                coefficients(j + SUB, strip[j + SUB])
                first[j + SUB, body, :] = tracer[0, j].astype(jnp.float32)
                return carry

            lax.fori_loop(0, six, load, 0)
            prepare()

        @pl.when(step == SUB)
        def _():
            def load(j, carry):
                coefficients(j, strip[width - SUB + j])
                first[j, body, :] = tracer[0, width - six + j].astype(jnp.float32)
                return carry

            lax.fori_loop(0, six, load, 0)
            for j in range(SUB):
                rows = jnp.where(flags[2] == 1, rim[1, j], strip[width + SUB + j])
                coefficients(six + j, jnp.where(flags[3] == 1, rows, 0.0))
                first[six + j, body, :] = halo_e[0, j].astype(jnp.float32)
            prepare()

        slot = SUB + lax.rem(step, SUB)
        column = jnp.where(step < SUB, step, step + width - 2 * SUB)
    else:
        @pl.when(step == 0)
        def _():
            def load(j, carry):
                coefficients(j, strip[j + SUB])
                first[j, body, :] = tracer[0, j].astype(jnp.float32)
                return carry

            lax.fori_loop(0, local, load, 0)
            prepare()

        slot = SUB + step
        column = slot

    kind_row = kinds[pl.ds(column, 1), :]
    rows_here = strip[column + SUB]

    @pl.when(level == 0)
    def _():
        which = lax.rem(lax.broadcasted_iota(jnp.int32, (3 * LAND_ROWS, ny), 0), LAND_ROWS)
        one_hot = jnp.where(which == kind_row, 1.0, 0.0).astype(jnp.bfloat16)
        speed = tn_dot(one_hot, settle[...])
        depth = tn_dot(three_parts(rows_here), selector(3 * levels))
        second[0, body, :] = depth / (depth + speed)

    @pl.when(level == 0)
    def _():
        for y in range(0, ny, chunk):
            now = moved(first, slot, y) * second[0, pl.ds(PAD + y, chunk), :]
            out[0, 0, pl.ds(y, chunk), :] = now
            rounded[pl.ds(y, chunk), :] = now.astype(jnp.bfloat16)

    @pl.when(level != 0)
    def _():
        for y in range(0, ny, chunk):
            now = moved(first, slot, y)
            out[0, 0, pl.ds(y, chunk), :] = now
            rounded[pl.ds(y, chunk), :] = now.astype(jnp.bfloat16)

    projected = lax.dot_general(
        table[...], rounded[...], (((1,), (1,)), ((), ())), preferred_element_type=jnp.float32
    )
    bin_row = bins[pl.ds(column, 1), :]
    half = NBIN * 2 * NW
    dry = jnp.zeros((2 * NW, ny), jnp.float32)
    wet = jnp.zeros((2 * NW, ny), jnp.float32)
    for k in range(NBIN):
        chosen = bin_row == k
        dry = dry + jnp.where(chosen, projected[2 * NW * k : 2 * NW * (k + 1)], 0.0)
        wet = wet + jnp.where(chosen, projected[half + 2 * NW * k : half + 2 * NW * (k + 1)], 0.0)
    moisture = strip[column + SUB, pl.ds(2 * levels + level, 1), :]
    thickness = strip[column + SUB, pl.ds(3 * levels + level, 1), :]
    growth = moisture / (1.0 - moisture)
    opt[0, 0] = (dry + growth * wet) * thickness


def chem_call(edge, extras, shared, earlier):
    tracer, strip, sun, bins, kinds, table, settle, light = shared
    levels, width, ny, species = tracer.shape
    local = 3 * SUB if edge else width
    steps = 2 * SUB if edge else width - 2 * SUB
    last = levels - 1

    if edge:
        def place(l, i):
            return (last - l, jnp.where(i < SUB, i, i + width - 2 * SUB), 0, 0)
    else:
        def place(l, i):
            return (last - l, i + SUB, 0, 0)

    def whole(l, i):
        return (last - l, 0, 0, 0)

    halo_spec = pl.BlockSpec((1, SUB, ny, species), whole)
    in_specs = [pl.BlockSpec((1, width, ny, species), whole)] + [VMEM_SPEC] * 6 + [SMEM_SPEC]
    aliases = {}
    if edge:
        in_specs = [SMEM_SPEC, VMEM_SPEC, halo_spec, halo_spec] + in_specs
        in_specs += [pl.BlockSpec(memory_space=pl.ANY)] * 2
        aliases = {len(in_specs) - 2: 0, len(in_specs) - 1: 1}
    cells = levels * local * ny * species
    return pl.pallas_call(
        functools.partial(chem_kernel, levels, width, edge),
        grid=(levels, steps),
        in_specs=in_specs,
        out_specs=[
            pl.BlockSpec((1, 1, ny, species), place),
            pl.BlockSpec((1, 1, 2 * NW, ny), place),
        ],
        out_shape=[
            jax.ShapeDtypeStruct((levels, width, ny, species), jnp.float32),
            jax.ShapeDtypeStruct((levels, width, 2 * NW, ny), jnp.float32),
        ],
        scratch_shapes=[
            pltpu.VMEM((local, ny + 2 * PAD, species), jnp.float32),
            pltpu.VMEM((local, ny + 2 * PAD, species), jnp.float32),
            pltpu.VMEM((local, ny, species), jnp.float32),
            pltpu.VMEM((local, ny, species), jnp.float32),
            pltpu.VMEM((ny, species), jnp.bfloat16),
        ],
        input_output_aliases=aliases,
        compiler_params=pltpu.CompilerParams(
            dimension_semantics=("arbitrary", "arbitrary"),
            vmem_limit_bytes=60 * 1024 * 1024,
        ),
        cost_estimate=pl.CostEstimate(
            flops=cells * 40, bytes_accessed=cells * 6, transcendentals=0
        ),
        name="edge_columns" if edge else "inner_columns",
    )(*extras, tracer, strip, sun, bins, kinds, table, settle, light, *earlier)


def radiate(optical, cosine, sunlight):
    overhead = jnp.zeros_like(optical[0, :, :NW])
    layers = [None] * optical.shape[0]
    for height in reversed(range(optical.shape[0])):
        transmitted = jnp.exp(-overhead / cosine[:, None])
        layers[height] = cosine * jnp.sum(
            sunlight[None, :, None] * optical[height, :, NW:] * transmitted, axis=1
        )
        overhead = overhead + optical[height, :, :NW]
    return jnp.stack(layers, axis=1)


def per_device(
    tracer_amounts,
    zonal_transit_ratio,
    meridional_transit_ratio,
    moisture_ratio,
    stratum_depths,
    sun_elevation_factor,
    thermal_anomaly,
    particle_class_map,
    ground_cover_kind,
    arid_extinction_table,
    swelling_factors,
    settling_velocities,
    arriving_irradiance,
):
    levels, width, ny, species = tracer_amounts.shape
    gx_count = lax.axis_size("gx")
    gy_count = lax.axis_size("gy")
    total = gx_count * gy_count
    gx = lax.axis_index("gx")
    gy = lax.axis_index("gy")
    tile_x, tile_y = sun_elevation_factor.shape
    both = ("gx", "gy")
    halo_w = lax.ppermute(
        tracer_amounts[:, width - SUB :], both, [(i, i + 1) for i in range(total - 1)]
    )
    halo_e = lax.ppermute(
        tracer_amounts[:, :SUB], both, [(i + 1, i) for i in range(total - 1)]
    )

    fields = jnp.concatenate(
        [zonal_transit_ratio, meridional_transit_ratio, moisture_ratio, stratum_depths], axis=0
    )
    field_count = fields.shape[0]
    fields = jnp.pad(fields.transpose(1, 0, 2), ((SUB, SUB), (0, 0), (0, 0)))
    t = thermal_anomaly
    span_y = max(tile_x, tile_y)

    def edge_rows(rows):
        return jnp.pad(rows, ((0, 8 - levels), (0, span_y - rows.shape[1])))

    fringe = jnp.stack(
        [edge_rows(t[:, 0]), edge_rows(t[:, -1]), edge_rows(t[:, :, 0]), edge_rows(t[:, :, -1])]
    )
    dma = pltpu.SemaphoreType.DMA
    strip, rim, strip_sun, fringe_in = pl.pallas_call(
        functools.partial(fields_kernel, gx_count, gy_count, width),
        in_specs=[VMEM_SPEC] * 3,
        out_specs=[VMEM_SPEC] * 4,
        out_shape=[
            jax.ShapeDtypeStruct((width + 2 * SUB, field_count, ny), jnp.float32),
            jax.ShapeDtypeStruct((2, SUB, field_count, ny), jnp.float32),
            jax.ShapeDtypeStruct((width, ny), jnp.float32),
            jax.ShapeDtypeStruct(fringe.shape, jnp.float32),
        ],
        scratch_shapes=[
            dma((gy_count,)), dma((gy_count,)), dma((gy_count,)), dma((gy_count,)),
            dma((2,)), dma((gy_count,)), dma((4,)), dma((4,)),
        ],
        compiler_params=pltpu.CompilerParams(collective_id=0, has_side_effects=True),
        name="field_exchange",
    )(fields, sun_elevation_factor, fringe)

    east_row = jnp.where(gx == gx_count - 1, 0.0, fringe_in[0, :levels, :tile_y])
    west_row = jnp.where(gx == 0, 0.0, fringe_in[1, :levels, :tile_y])
    north_col = jnp.where(gy == gy_count - 1, 0.0, fringe_in[2, :levels, :tile_x])
    south_col = jnp.where(gy == 0, 0.0, fringe_in[3, :levels, :tile_x])
    wide_x = jnp.concatenate([west_row[:, None], t, east_row[:, None]], axis=1)
    wide_y = jnp.concatenate([south_col[:, :, None], t, north_col[:, :, None]], axis=2)
    laplace = wide_x[:, 2:] + wide_x[:, :-2] + wide_y[:, :, 2:] + wide_y[:, :, :-2] - 4.0 * t
    base = t + SPREAD_FACTOR * laplace

    table = jnp.concatenate([arid_extinction_table, swelling_factors], axis=1).T
    land = jnp.pad(
        settling_velocities, ((0, LAND_ROWS - settling_velocities.shape[0]), (0, 0))
    )
    high = lax.reduce_precision(land, 8, 7)
    middle = lax.reduce_precision(land - high, 8, 7)
    settle = jnp.concatenate([high, middle, land - high - middle], axis=0).astype(jnp.bfloat16)
    shared = (
        tracer_amounts, strip, strip_sun, particle_class_map, ground_cover_kind,
        table, settle, arriving_irradiance,
    )
    updated, optical = chem_call(False, (), shared, ())
    flags = jnp.stack(
        [gy == 0, (gx > 0) | (gy > 0), gy == gy_count - 1, (gx < gx_count - 1) | (gy < gy_count - 1)]
    ).astype(jnp.int32)
    updated, optical = chem_call(
        True, (flags, rim, halo_w, halo_e), shared, (updated, optical)
    )
    heat = radiate(optical, strip_sun, arriving_irradiance)
    anomaly = pl.pallas_call(
        functools.partial(return_kernel, gx_count, gy_count, width),
        in_specs=[VMEM_SPEC] * 2,
        out_specs=VMEM_SPEC,
        out_shape=jax.ShapeDtypeStruct(t.shape, jnp.float32),
        scratch_shapes=[
            pltpu.VMEM((tile_x, levels, tile_y), jnp.float32),
            dma((gy_count,)), dma((gy_count,)),
        ],
        compiler_params=pltpu.CompilerParams(collective_id=1, has_side_effects=True),
        name="heat_return",
    )(heat, base)
    return (updated, anomaly)


def solution(mesh):
    return jax.shard_map(
        per_device,
        mesh=mesh,
        in_specs=(
            P(None, ("gx", "gy"), None, None),
            P(None, "gx", "gy"),
            P(None, "gx", "gy"),
            P(None, "gx", "gy"),
            P(None, "gx", "gy"),
            P("gx", "gy"),
            P(None, "gx", "gy"),
            P(("gx", "gy"), None),
            P(("gx", "gy"), None),
            P(),
            P(),
            P(),
            P(),
        ),
        out_specs=(P(None, ("gx", "gy"), None, None), P(None, "gx", "gy")),
        check_vma=False,
    )
```

```python
import functools

import jax
import jax.numpy as jnp
from jax import lax
from jax.experimental import pallas as pl
from jax.experimental.pallas import tpu as pltpu
from jax.sharding import PartitionSpec as P

SUB = 3
NBIN = 8
NW = 4
SPREAD_FACTOR = 0.2
PAD = 8
LAND_ROWS = 32
MESH = pl.DeviceIdType.MESH
VMEM_SPEC = pl.BlockSpec(memory_space=pltpu.VMEM)
SMEM_SPEC = pl.BlockSpec(memory_space=pltpu.SMEM)


def greet(gx_count, gy_count, reach):
    gx = lax.axis_index("gx")
    gy = lax.axis_index("gy")
    barrier = pltpu.get_barrier_semaphore()
    for dx in range(-reach, reach + 1):
        for dy in range(gy_count):
            if dx == 0 and dy == 0:
                continue
            pl.semaphore_signal(
                barrier,
                inc=1,
                device_id=(
                    lax.rem(gx + dx + gx_count, gx_count),
                    lax.rem(gy + dy, gy_count),
                ),
                device_id_type=MESH,
            )
    pl.semaphore_wait(barrier, (2 * reach + 1) * gy_count - 1)


def fields_kernel(
    gx_count, gy_count, width,
    fields, sun, fringe,
    strip, rim, strip_sun, fringe_in,
    send_a, recv_a, send_s, recv_s, send_r, recv_r, send_f, recv_f,
):
    gx = lax.axis_index("gx")
    gy = lax.axis_index("gy")
    span = width + 2 * SUB
    tile_x = width * gy_count
    tile_y = fields.shape[2]
    right = lax.rem(gx + 1, gx_count)
    left = lax.rem(gx + gx_count - 1, gx_count)
    up = lax.rem(gy + 1, gy_count)
    down = lax.rem(gy + gy_count - 1, gy_count)
    greet(gx_count, gy_count, 1)
    mine = pl.ds(pl.multiple_of(gy * tile_y, tile_y), tile_y)

    def rims(side):
        lo = tile_x if side == 0 else SUB
        return pltpu.make_async_remote_copy(
            src_ref=fields.at[pl.ds(lo, SUB)],
            dst_ref=rim.at[side, :, :, mine],
            send_sem=send_r.at[side],
            recv_sem=recv_r.at[gy],
            device_id=((right, 0) if side == 0 else (left, gy_count - 1)),
            device_id_type=MESH,
        )

    def slab(peer):
        return pltpu.make_async_remote_copy(
            src_ref=fields.at[pl.ds(peer * width, span)],
            dst_ref=strip.at[:, :, mine],
            send_sem=send_a.at[peer],
            recv_sem=recv_a.at[gy],
            device_id=(gx, peer),
            device_id_type=MESH,
        )

    def sunny(peer):
        return pltpu.make_async_remote_copy(
            src_ref=sun.at[pl.ds(peer * width, width)],
            dst_ref=strip_sun.at[:, mine],
            send_sem=send_s.at[peer],
            recv_sem=recv_s.at[gy],
            device_id=(gx, peer),
            device_id_type=MESH,
        )

    targets = ((left, gy), (right, gy), (gx, down), (gx, up))
    edges = [
        pltpu.make_async_remote_copy(
            src_ref=fringe.at[k],
            dst_ref=fringe_in.at[k],
            send_sem=send_f.at[k],
            recv_sem=recv_f.at[k],
            device_id=targets[k],
            device_id_type=MESH,
        )
        for k in range(4)
    ]
    for peer in range(gy_count):
        @pl.when(gy != peer)
        def _(peer=peer):
            slab(peer).start()
            sunny(peer).start()
    for side in range(2):
        rims(side).start()
    for edge in edges:
        edge.start()
    strip[:, :, mine] = fields[pl.ds(gy * width, span)]
    strip_sun[:, mine] = sun[pl.ds(pl.multiple_of(gy * width, width), width), :]
    for edge in edges:
        edge.wait()
    for side in range(2):
        rims(side).wait_send()
    for peer in range(gy_count):
        @pl.when(gy != peer)
        def _(peer=peer):
            slab(peer).wait_send()
            sunny(peer).wait_send()
            theirs = pl.ds(peer * tile_y, tile_y)
            pltpu.make_async_remote_copy(
                src_ref=fields.at[pl.ds(0, span)],
                dst_ref=strip.at[:, :, theirs],
                send_sem=send_a.at[peer],
                recv_sem=recv_a.at[peer],
                device_id=(gx, peer),
                device_id_type=MESH,
            ).wait_recv()
            pltpu.make_async_remote_copy(
                src_ref=sun.at[pl.ds(0, width)],
                dst_ref=strip_sun.at[:, theirs],
                send_sem=send_s.at[peer],
                recv_sem=recv_s.at[peer],
                device_id=(gx, peer),
                device_id_type=MESH,
            ).wait_recv()
    for side, owner, source in ((0, 0, left), (1, gy_count - 1, right)):
        @pl.when(gy == owner)
        def _(side=side, source=source):
            for peer in range(gy_count):
                pltpu.make_async_remote_copy(
                    src_ref=fields.at[pl.ds(0, SUB)],
                    dst_ref=rim.at[side, :, :, pl.ds(peer * tile_y, tile_y)],
                    send_sem=send_r.at[side],
                    recv_sem=recv_r.at[peer],
                    device_id=(source, peer),
                    device_id_type=MESH,
                ).wait_recv()


def return_kernel(
    gx_count, gy_count, width, heat, base, out, tile, send_sem, recv_sem
):
    gx = lax.axis_index("gx")
    gy = lax.axis_index("gy")
    tile_y = base.shape[2]
    greet(gx_count, gy_count, 0)

    def slab(peer):
        return pltpu.make_async_remote_copy(
            src_ref=heat.at[:, :, pl.ds(peer * tile_y, tile_y)],
            dst_ref=tile.at[pl.ds(gy * width, width)],
            send_sem=send_sem.at[peer],
            recv_sem=recv_sem.at[gy],
            device_id=(gx, peer),
            device_id_type=MESH,
        )

    for peer in range(gy_count):
        @pl.when(gy != peer)
        def _(peer=peer):
            slab(peer).start()
    mine = pl.ds(pl.multiple_of(gy * tile_y, tile_y), tile_y)
    tile[pl.ds(gy * width, width)] = heat[:, :, mine]
    for peer in range(gy_count):
        @pl.when(gy != peer)
        def _(peer=peer):
            slab(peer).wait_send()
            pltpu.make_async_remote_copy(
                src_ref=heat.at[:, :, pl.ds(0, tile_y)],
                dst_ref=tile.at[pl.ds(peer * width, width)],
                send_sem=send_sem.at[peer],
                recv_sem=recv_sem.at[peer],
                device_id=(gx, peer),
                device_id_type=MESH,
            ).wait_recv()
    for level in range(base.shape[0]):
        out[level] = base[level] + tile[:, level, :]


def tn_dot(left, right):
    return lax.dot_general(
        left, right, (((0,), (0,)), ((), ())), preferred_element_type=jnp.float32
    )


def three_parts(rows):
    high = rows.astype(jnp.bfloat16).astype(jnp.float32)
    rest = rows - high
    middle = rest.astype(jnp.bfloat16).astype(jnp.float32)
    return jnp.concatenate([high, middle, rest - middle], axis=0).astype(jnp.bfloat16)


def chem_kernel(levels, width, edge, *refs):
    if edge:
        (flags, rim, halo_w, halo_e, tracer, strip, sun, bins, kinds, table, settle, light,
         _out_in, _opt_in, out, opt, first, second, zonal, merid, rounded) = refs
    else:
        (tracer, strip, sun, bins, kinds, table, settle, light,
         out, opt, first, second, zonal, merid, rounded) = refs
    level = levels - 1 - pl.program_id(0)
    step = pl.program_id(1)
    ny = tracer.shape[2]
    fields = strip.shape[1]
    local = first.shape[0]
    chunk = 64

    def selector(row):
        which = lax.rem(lax.broadcasted_iota(jnp.int32, (3 * fields, 128), 0), fields)
        return jnp.where(which == row, 1.0, 0.0).astype(jnp.bfloat16)

    def coefficients(slot, rows):
        parts = three_parts(rows)
        zonal[slot] = tn_dot(parts, selector(level))
        merid[slot] = tn_dot(parts, selector(levels + level))

    def moved(source, slot, y):
        here = source[slot, pl.ds(PAD + y, chunk), :]
        c = zonal[slot, pl.ds(y, chunk), :]
        d = merid[slot, pl.ds(y, chunk), :]
        across = jnp.where(
            c > 0.0,
            source[slot - 1, pl.ds(PAD + y, chunk), :],
            source[slot + 1, pl.ds(PAD + y, chunk), :],
        )
        along = jnp.where(
            d > 0.0,
            source[slot, pl.ds(PAD - 1 + y, chunk), :],
            source[slot, pl.ds(PAD + 1 + y, chunk), :],
        )
        return here + jnp.abs(c) * (across - here) + jnp.abs(d) * (along - here)

    def advance(source, target, low, high):
        def column(slot, carry):
            for y in range(0, ny, chunk):
                target[slot, pl.ds(PAD + y, chunk), :] = moved(source, slot, y)
            return carry

        lax.fori_loop(low, high, column, 0)

    def prepare():
        advance(first, second, 1, local - 1)
        advance(second, first, 2, local - 2)

    @pl.when((pl.program_id(0) == 0) & (step == 0))
    def _():
        zeros = jnp.zeros((local, PAD, 128), jnp.float32)
        for buffer in (first, second):
            buffer[:, pl.ds(0, PAD), :] = zeros
            buffer[:, pl.ds(PAD + ny, PAD), :] = zeros

    body = pl.ds(PAD, ny)
    if edge:
        six = local - SUB

        @pl.when(step == 0)
        def _():
            for j in range(SUB):
                rows = jnp.where(flags[0] == 1, rim[0, j], strip[j])
                coefficients(j, jnp.where(flags[1] == 1, rows, 0.0))
                first[j, body, :] = halo_w[0, j].astype(jnp.float32)

            def load(j, carry):
                coefficients(j + SUB, strip[j + SUB])
                first[j + SUB, body, :] = tracer[0, j].astype(jnp.float32)
                return carry

            lax.fori_loop(0, six, load, 0)
            prepare()

        @pl.when(step == SUB)
        def _():
            def load(j, carry):
                coefficients(j, strip[width - SUB + j])
                first[j, body, :] = tracer[0, width - six + j].astype(jnp.float32)
                return carry

            lax.fori_loop(0, six, load, 0)
            for j in range(SUB):
                rows = jnp.where(flags[2] == 1, rim[1, j], strip[width + SUB + j])
                coefficients(six + j, jnp.where(flags[3] == 1, rows, 0.0))
                first[six + j, body, :] = halo_e[0, j].astype(jnp.float32)
            prepare()

        slot = SUB + lax.rem(step, SUB)
        column = jnp.where(step < SUB, step, step + width - 2 * SUB)
    else:
        @pl.when(step == 0)
        def _():
            def load(j, carry):
                coefficients(j, strip[j + SUB])
                first[j, body, :] = tracer[0, j].astype(jnp.float32)
                return carry

            lax.fori_loop(0, local, load, 0)
            prepare()

        slot = SUB + step
        column = slot

    kind_row = kinds[pl.ds(column, 1), :]
    rows_here = strip[column + SUB]

    @pl.when(level == 0)
    def _():
        which = lax.rem(lax.broadcasted_iota(jnp.int32, (3 * LAND_ROWS, ny), 0), LAND_ROWS)
        one_hot = jnp.where(which == kind_row, 1.0, 0.0).astype(jnp.bfloat16)
        speed = tn_dot(one_hot, settle[...])
        depth = tn_dot(three_parts(rows_here), selector(3 * levels))
        second[0, body, :] = depth / (depth + speed)

    @pl.when(level == 0)
    def _():
        for y in range(0, ny, chunk):
            now = moved(first, slot, y) * second[0, pl.ds(PAD + y, chunk), :]
            out[0, 0, pl.ds(y, chunk), :] = now
            rounded[pl.ds(y, chunk), :] = now.astype(jnp.bfloat16)

    @pl.when(level != 0)
    def _():
        for y in range(0, ny, chunk):
            now = moved(first, slot, y)
            out[0, 0, pl.ds(y, chunk), :] = now
            rounded[pl.ds(y, chunk), :] = now.astype(jnp.bfloat16)

    projected = lax.dot_general(
        table[...], rounded[...], (((1,), (1,)), ((), ())), preferred_element_type=jnp.float32
    )
    bin_row = bins[pl.ds(column, 1), :]
    half = NBIN * 2 * NW
    dry = jnp.zeros((2 * NW, ny), jnp.float32)
    wet = jnp.zeros((2 * NW, ny), jnp.float32)
    for k in range(NBIN):
        chosen = bin_row == k
        dry = dry + jnp.where(chosen, projected[2 * NW * k : 2 * NW * (k + 1)], 0.0)
        wet = wet + jnp.where(chosen, projected[half + 2 * NW * k : half + 2 * NW * (k + 1)], 0.0)
    moisture = strip[column + SUB, pl.ds(2 * levels + level, 1), :]
    thickness = strip[column + SUB, pl.ds(3 * levels + level, 1), :]
    growth = moisture / (1.0 - moisture)
    opt[0, 0] = (dry + growth * wet) * thickness


def chem_call(edge, extras, shared, earlier):
    tracer, strip, sun, bins, kinds, table, settle, light = shared
    levels, width, ny, species = tracer.shape
    local = 3 * SUB if edge else width
    steps = 2 * SUB if edge else width - 2 * SUB
    last = levels - 1

    if edge:
        def place(l, i):
            return (last - l, jnp.where(i < SUB, i, i + width - 2 * SUB), 0, 0)
    else:
        def place(l, i):
            return (last - l, i + SUB, 0, 0)

    def whole(l, i):
        return (last - l, 0, 0, 0)

    halo_spec = pl.BlockSpec((1, SUB, ny, species), whole)
    in_specs = [pl.BlockSpec((1, width, ny, species), whole)] + [VMEM_SPEC] * 6 + [SMEM_SPEC]
    aliases = {}
    if edge:
        in_specs = [SMEM_SPEC, VMEM_SPEC, halo_spec, halo_spec] + in_specs
        in_specs += [pl.BlockSpec(memory_space=pl.ANY)] * 2
        aliases = {len(in_specs) - 2: 0, len(in_specs) - 1: 1}
    cells = levels * local * ny * species
    return pl.pallas_call(
        functools.partial(chem_kernel, levels, width, edge),
        grid=(levels, steps),
        in_specs=in_specs,
        out_specs=[
            pl.BlockSpec((1, 1, ny, species), place),
            pl.BlockSpec((1, 1, 2 * NW, ny), place),
        ],
        out_shape=[
            jax.ShapeDtypeStruct((levels, width, ny, species), jnp.float32),
            jax.ShapeDtypeStruct((levels, width, 2 * NW, ny), jnp.float32),
        ],
        scratch_shapes=[
            pltpu.VMEM((local, ny + 2 * PAD, species), jnp.float32),
            pltpu.VMEM((local, ny + 2 * PAD, species), jnp.float32),
            pltpu.VMEM((local, ny, species), jnp.float32),
            pltpu.VMEM((local, ny, species), jnp.float32),
            pltpu.VMEM((ny, species), jnp.bfloat16),
        ],
        input_output_aliases=aliases,
        compiler_params=pltpu.CompilerParams(
            dimension_semantics=("arbitrary", "arbitrary"),
            vmem_limit_bytes=60 * 1024 * 1024,
        ),
        cost_estimate=pl.CostEstimate(
            flops=cells * 40, bytes_accessed=cells * 6, transcendentals=0
        ),
        name="edge_columns" if edge else "inner_columns",
    )(*extras, tracer, strip, sun, bins, kinds, table, settle, light, *earlier)


def radiate(optical, cosine, sunlight):
    overhead = jnp.zeros_like(optical[0, :, :NW])
    layers = [None] * optical.shape[0]
    for height in reversed(range(optical.shape[0])):
        transmitted = jnp.exp(-overhead / cosine[:, None])
        layers[height] = cosine * jnp.sum(
            sunlight[None, :, None] * optical[height, :, NW:] * transmitted, axis=1
        )
        overhead = overhead + optical[height, :, :NW]
    return jnp.stack(layers, axis=1)


def per_device(
    tracer_amounts,
    zonal_transit_ratio,
    meridional_transit_ratio,
    moisture_ratio,
    stratum_depths,
    sun_elevation_factor,
    thermal_anomaly,
    particle_class_map,
    ground_cover_kind,
    arid_extinction_table,
    swelling_factors,
    settling_velocities,
    arriving_irradiance,
):
    levels, width, ny, species = tracer_amounts.shape
    gx_count = lax.axis_size("gx")
    gy_count = lax.axis_size("gy")
    total = gx_count * gy_count
    gx = lax.axis_index("gx")
    gy = lax.axis_index("gy")
    tile_x, tile_y = sun_elevation_factor.shape
    both = ("gx", "gy")
    fields = jnp.concatenate(
        [zonal_transit_ratio, meridional_transit_ratio, moisture_ratio, stratum_depths], axis=0
    )
    field_count = fields.shape[0]
    fields = jnp.pad(fields.transpose(1, 0, 2), ((SUB, SUB), (0, 0), (0, 0)))
    t = thermal_anomaly
    span_y = max(tile_x, tile_y)

    def edge_rows(rows):
        return jnp.pad(rows, ((0, 8 - levels), (0, span_y - rows.shape[1])))

    fringe = jnp.stack(
        [edge_rows(t[:, 0]), edge_rows(t[:, -1]), edge_rows(t[:, :, 0]), edge_rows(t[:, :, -1])]
    )
    dma = pltpu.SemaphoreType.DMA
    strip, rim, strip_sun, fringe_in = pl.pallas_call(
        functools.partial(fields_kernel, gx_count, gy_count, width),
        in_specs=[VMEM_SPEC] * 3,
        out_specs=[VMEM_SPEC] * 4,
        out_shape=[
            jax.ShapeDtypeStruct((width + 2 * SUB, field_count, ny), jnp.float32),
            jax.ShapeDtypeStruct((2, SUB, field_count, ny), jnp.float32),
            jax.ShapeDtypeStruct((width, ny), jnp.float32),
            jax.ShapeDtypeStruct(fringe.shape, jnp.float32),
        ],
        scratch_shapes=[
            dma((gy_count,)), dma((gy_count,)), dma((gy_count,)), dma((gy_count,)),
            dma((2,)), dma((gy_count,)), dma((4,)), dma((4,)),
        ],
        compiler_params=pltpu.CompilerParams(collective_id=0, has_side_effects=True),
        name="field_exchange",
    )(fields, sun_elevation_factor, fringe)

    tail, head, strip = lax.optimization_barrier(
        (tracer_amounts[:, width - SUB :], tracer_amounts[:, :SUB], strip)
    )
    halo_w = lax.ppermute(tail, both, [(i, i + 1) for i in range(total - 1)])
    halo_e = lax.ppermute(head, both, [(i + 1, i) for i in range(total - 1)])

    east_row = jnp.where(gx == gx_count - 1, 0.0, fringe_in[0, :levels, :tile_y])
    west_row = jnp.where(gx == 0, 0.0, fringe_in[1, :levels, :tile_y])
    north_col = jnp.where(gy == gy_count - 1, 0.0, fringe_in[2, :levels, :tile_x])
    south_col = jnp.where(gy == 0, 0.0, fringe_in[3, :levels, :tile_x])
    wide_x = jnp.concatenate([west_row[:, None], t, east_row[:, None]], axis=1)
    wide_y = jnp.concatenate([south_col[:, :, None], t, north_col[:, :, None]], axis=2)
    laplace = wide_x[:, 2:] + wide_x[:, :-2] + wide_y[:, :, 2:] + wide_y[:, :, :-2] - 4.0 * t
    base = t + SPREAD_FACTOR * laplace

    table = jnp.concatenate([arid_extinction_table, swelling_factors], axis=1).T
    land = jnp.pad(
        settling_velocities, ((0, LAND_ROWS - settling_velocities.shape[0]), (0, 0))
    )
    high = lax.reduce_precision(land, 8, 7)
    middle = lax.reduce_precision(land - high, 8, 7)
    settle = jnp.concatenate([high, middle, land - high - middle], axis=0).astype(jnp.bfloat16)
    shared = (
        tracer_amounts, strip, strip_sun, particle_class_map, ground_cover_kind,
        table, settle, arriving_irradiance,
    )
    updated, optical = chem_call(False, (), shared, ())
    flags = jnp.stack(
        [gy == 0, (gx > 0) | (gy > 0), gy == gy_count - 1, (gx < gx_count - 1) | (gy < gy_count - 1)]
    ).astype(jnp.int32)
    updated, optical = chem_call(
        True, (flags, rim, halo_w, halo_e), shared, (updated, optical)
    )
    heat = radiate(optical, strip_sun, arriving_irradiance)
    anomaly = pl.pallas_call(
        functools.partial(return_kernel, gx_count, gy_count, width),
        in_specs=[VMEM_SPEC] * 2,
        out_specs=VMEM_SPEC,
        out_shape=jax.ShapeDtypeStruct(t.shape, jnp.float32),
        scratch_shapes=[
            pltpu.VMEM((tile_x, levels, tile_y), jnp.float32),
            dma((gy_count,)), dma((gy_count,)),
        ],
        compiler_params=pltpu.CompilerParams(collective_id=1, has_side_effects=True),
        name="heat_return",
    )(heat, base)
    return (updated, anomaly)


def solution(mesh):
    return jax.shard_map(
        per_device,
        mesh=mesh,
        in_specs=(
            P(None, ("gx", "gy"), None, None),
            P(None, "gx", "gy"),
            P(None, "gx", "gy"),
            P(None, "gx", "gy"),
            P(None, "gx", "gy"),
            P("gx", "gy"),
            P(None, "gx", "gy"),
            P(("gx", "gy"), None),
            P(("gx", "gy"), None),
            P(),
            P(),
            P(),
            P(),
        ),
        out_specs=(P(None, ("gx", "gy"), None, None), P(None, "gx", "gy")),
        check_vma=False,
    )
```

```python
import functools

import jax
import jax.numpy as jnp
from jax import lax
from jax.experimental import pallas as pl
from jax.experimental.pallas import tpu as pltpu
from jax.sharding import PartitionSpec as P

SUB = 3
NBIN = 8
NW = 4
SPREAD_FACTOR = 0.2
PAD = 8
LAND_ROWS = 32
MESH = pl.DeviceIdType.MESH
VMEM_SPEC = pl.BlockSpec(memory_space=pltpu.VMEM)
SMEM_SPEC = pl.BlockSpec(memory_space=pltpu.SMEM)


def greet(gx_count, gy_count, reach):
    gx = lax.axis_index("gx")
    gy = lax.axis_index("gy")
    barrier = pltpu.get_barrier_semaphore()
    for dx in range(-reach, reach + 1):
        for dy in range(gy_count):
            if dx == 0 and dy == 0:
                continue
            pl.semaphore_signal(
                barrier,
                inc=1,
                device_id=(
                    lax.rem(gx + dx + gx_count, gx_count),
                    lax.rem(gy + dy, gy_count),
                ),
                device_id_type=MESH,
            )
    pl.semaphore_wait(barrier, (2 * reach + 1) * gy_count - 1)


def fields_kernel(
    gx_count, gy_count, width,
    fields, sun, fringe,
    strip, rim, strip_sun, fringe_in,
    send_a, recv_a, send_s, recv_s, send_r, recv_r, send_f, recv_f,
):
    gx = lax.axis_index("gx")
    gy = lax.axis_index("gy")
    span = width + 2 * SUB
    tile_x = width * gy_count
    tile_y = fields.shape[2]
    right = lax.rem(gx + 1, gx_count)
    left = lax.rem(gx + gx_count - 1, gx_count)
    up = lax.rem(gy + 1, gy_count)
    down = lax.rem(gy + gy_count - 1, gy_count)
    greet(gx_count, gy_count, 1)
    mine = pl.ds(pl.multiple_of(gy * tile_y, tile_y), tile_y)

    def rims(side):
        lo = tile_x if side == 0 else SUB
        return pltpu.make_async_remote_copy(
            src_ref=fields.at[pl.ds(lo, SUB)],
            dst_ref=rim.at[side, :, :, mine],
            send_sem=send_r.at[side],
            recv_sem=recv_r.at[gy],
            device_id=((right, 0) if side == 0 else (left, gy_count - 1)),
            device_id_type=MESH,
        )

    def slab(peer):
        return pltpu.make_async_remote_copy(
            src_ref=fields.at[pl.ds(peer * width, span)],
            dst_ref=strip.at[:, :, mine],
            send_sem=send_a.at[peer],
            recv_sem=recv_a.at[gy],
            device_id=(gx, peer),
            device_id_type=MESH,
        )

    def sunny(peer):
        return pltpu.make_async_remote_copy(
            src_ref=sun.at[pl.ds(peer * width, width)],
            dst_ref=strip_sun.at[:, mine],
            send_sem=send_s.at[peer],
            recv_sem=recv_s.at[gy],
            device_id=(gx, peer),
            device_id_type=MESH,
        )

    targets = ((left, gy), (right, gy), (gx, down), (gx, up))
    edges = [
        pltpu.make_async_remote_copy(
            src_ref=fringe.at[k],
            dst_ref=fringe_in.at[k],
            send_sem=send_f.at[k],
            recv_sem=recv_f.at[k],
            device_id=targets[k],
            device_id_type=MESH,
        )
        for k in range(4)
    ]
    for peer in range(gy_count):
        @pl.when(gy != peer)
        def _(peer=peer):
            slab(peer).start()
            sunny(peer).start()
    for side in range(2):
        rims(side).start()
    for edge in edges:
        edge.start()
    strip[:, :, mine] = fields[pl.ds(gy * width, span)]
    strip_sun[:, mine] = sun[pl.ds(pl.multiple_of(gy * width, width), width), :]
    for edge in edges:
        edge.wait()
    for side in range(2):
        rims(side).wait_send()
    for peer in range(gy_count):
        @pl.when(gy != peer)
        def _(peer=peer):
            slab(peer).wait_send()
            sunny(peer).wait_send()
            theirs = pl.ds(peer * tile_y, tile_y)
            pltpu.make_async_remote_copy(
                src_ref=fields.at[pl.ds(0, span)],
                dst_ref=strip.at[:, :, theirs],
                send_sem=send_a.at[peer],
                recv_sem=recv_a.at[peer],
                device_id=(gx, peer),
                device_id_type=MESH,
            ).wait_recv()
            pltpu.make_async_remote_copy(
                src_ref=sun.at[pl.ds(0, width)],
                dst_ref=strip_sun.at[:, theirs],
                send_sem=send_s.at[peer],
                recv_sem=recv_s.at[peer],
                device_id=(gx, peer),
                device_id_type=MESH,
            ).wait_recv()
    for side, owner, source in ((0, 0, left), (1, gy_count - 1, right)):
        @pl.when(gy == owner)
        def _(side=side, source=source):
            for peer in range(gy_count):
                pltpu.make_async_remote_copy(
                    src_ref=fields.at[pl.ds(0, SUB)],
                    dst_ref=rim.at[side, :, :, pl.ds(peer * tile_y, tile_y)],
                    send_sem=send_r.at[side],
                    recv_sem=recv_r.at[peer],
                    device_id=(source, peer),
                    device_id_type=MESH,
                ).wait_recv()


def return_kernel(
    gx_count, gy_count, width, heat, base, out, tile, send_sem, recv_sem
):
    gx = lax.axis_index("gx")
    gy = lax.axis_index("gy")
    tile_y = base.shape[2]
    greet(gx_count, gy_count, 0)

    def slab(peer):
        return pltpu.make_async_remote_copy(
            src_ref=heat.at[:, :, pl.ds(peer * tile_y, tile_y)],
            dst_ref=tile.at[pl.ds(gy * width, width)],
            send_sem=send_sem.at[peer],
            recv_sem=recv_sem.at[gy],
            device_id=(gx, peer),
            device_id_type=MESH,
        )

    for peer in range(gy_count):
        @pl.when(gy != peer)
        def _(peer=peer):
            slab(peer).start()
    mine = pl.ds(pl.multiple_of(gy * tile_y, tile_y), tile_y)
    tile[pl.ds(gy * width, width)] = heat[:, :, mine]
    for peer in range(gy_count):
        @pl.when(gy != peer)
        def _(peer=peer):
            slab(peer).wait_send()
            pltpu.make_async_remote_copy(
                src_ref=heat.at[:, :, pl.ds(0, tile_y)],
                dst_ref=tile.at[pl.ds(peer * width, width)],
                send_sem=send_sem.at[peer],
                recv_sem=recv_sem.at[peer],
                device_id=(gx, peer),
                device_id_type=MESH,
            ).wait_recv()
    for level in range(base.shape[0]):
        out[level] = base[level] + tile[:, level, :]


def tn_dot(left, right):
    return lax.dot_general(
        left, right, (((0,), (0,)), ((), ())), preferred_element_type=jnp.float32
    )


def three_parts(rows):
    high = rows.astype(jnp.bfloat16).astype(jnp.float32)
    rest = rows - high
    middle = rest.astype(jnp.bfloat16).astype(jnp.float32)
    return jnp.concatenate([high, middle, rest - middle], axis=0).astype(jnp.bfloat16)


def chem_kernel(levels, width, edge, *refs):
    if edge:
        (flags, rim, halo_w, halo_e, saved, near_w, near_e, strip, bins, kinds, table, settle,
         _out_in, _opt_in, out, opt, first, second, zonal, merid, rounded) = refs
    else:
        (tracer, strip, bins, kinds, table, settle,
         out, opt, saved, first, second, zonal, merid, rounded) = refs
    level = levels - 1 - pl.program_id(0)
    step = pl.program_id(1)
    ny = strip.shape[2]
    fields = strip.shape[1]
    local = first.shape[0]
    chunk = 64

    def selector(row):
        which = lax.rem(lax.broadcasted_iota(jnp.int32, (3 * fields, 128), 0), fields)
        return jnp.where(which == row, 1.0, 0.0).astype(jnp.bfloat16)

    def coefficients(slot, rows):
        parts = three_parts(rows)
        zonal[slot] = tn_dot(parts, selector(level))
        merid[slot] = tn_dot(parts, selector(levels + level))

    def moved(source, slot, y):
        here = source[slot, pl.ds(PAD + y, chunk), :]
        c = zonal[slot, pl.ds(y, chunk), :]
        d = merid[slot, pl.ds(y, chunk), :]
        across = jnp.where(
            c > 0.0,
            source[slot - 1, pl.ds(PAD + y, chunk), :],
            source[slot + 1, pl.ds(PAD + y, chunk), :],
        )
        along = jnp.where(
            d > 0.0,
            source[slot, pl.ds(PAD - 1 + y, chunk), :],
            source[slot, pl.ds(PAD + 1 + y, chunk), :],
        )
        return here + jnp.abs(c) * (across - here) + jnp.abs(d) * (along - here)

    def advance(source, target, low, high):
        def column(slot, carry):
            for y in range(0, ny, chunk):
                target[slot, pl.ds(PAD + y, chunk), :] = moved(source, slot, y)
            return carry

        lax.fori_loop(low, high, column, 0)

    @pl.when((pl.program_id(0) == 0) & (step == 0))
    def _():
        zeros = jnp.zeros((local, PAD, 128), jnp.float32)
        for buffer in (first, second):
            buffer[:, pl.ds(0, PAD), :] = zeros
            buffer[:, pl.ds(PAD + ny, PAD), :] = zeros

    body = pl.ds(PAD, ny)
    if edge:
        @pl.when(step == 0)
        def _():
            for j in (1, 2):
                rows = jnp.where(flags[0] == 1, rim[0, j], strip[j])
                coefficients(j, jnp.where(flags[1] == 1, rows, 0.0))
            for j in (3, 4, 5):
                coefficients(j, strip[j])
            for j in range(SUB):
                first[j, body, :] = halo_w[0, j].astype(jnp.float32)
            for j in range(2):
                first[SUB + j, body, :] = near_w[0, j].astype(jnp.float32)
                second[SUB + 1 + j, body, :] = saved[0, j]
            advance(first, second, 1, 4)
            advance(second, first, 2, 5)
            for j in range(2):
                first[SUB + 2 + j, body, :] = saved[0, 2 + j]

        @pl.when(step == SUB)
        def _():
            for j in (1, 2, 3):
                coefficients(j, strip[width - 1 + j])
            for j in (4, 5):
                rows = jnp.where(flags[2] == 1, rim[1, j - 4], strip[width - 1 + j])
                coefficients(j, jnp.where(flags[3] == 1, rows, 0.0))
            for j in range(SUB):
                first[4 + j, body, :] = halo_e[0, j].astype(jnp.float32)
            for j in range(2):
                first[2 + j, body, :] = near_e[0, j].astype(jnp.float32)
                second[1 + j, body, :] = saved[0, 4 + j]
            advance(first, second, 3, 6)
            advance(second, first, 2, 5)
            for j in range(2):
                first[j, body, :] = saved[0, 6 + j]

        slot = jnp.where(step < SUB, step + SUB, step - 2)
        column = jnp.where(step < SUB, step, step + width - 2 * SUB)
    else:
        @pl.when(step == 0)
        def _():
            def load(j, carry):
                coefficients(j, strip[j + SUB])
                first[j, body, :] = tracer[0, j].astype(jnp.float32)
                return carry

            lax.fori_loop(0, local, load, 0)
            advance(first, second, 1, local - 1)
            advance(second, first, 2, local - 2)
            kept = (
                (second, 1), (second, 2), (first, 2), (first, 3),
                (second, local - 3), (second, local - 2), (first, local - 4), (first, local - 3),
            )
            for k, (buffer, place) in enumerate(kept):
                saved[0, k] = buffer[place, body, :]

        slot = SUB + step
        column = slot

    kind_row = kinds[pl.ds(column, 1), :]
    rows_here = strip[column + SUB]

    @pl.when(level == 0)
    def _():
        which = lax.rem(lax.broadcasted_iota(jnp.int32, (3 * LAND_ROWS, ny), 0), LAND_ROWS)
        one_hot = jnp.where(which == kind_row, 1.0, 0.0).astype(jnp.bfloat16)
        speed = tn_dot(one_hot, settle[...])
        depth = tn_dot(three_parts(rows_here), selector(3 * levels))
        second[0, body, :] = depth / (depth + speed)

    @pl.when(level == 0)
    def _():
        for y in range(0, ny, chunk):
            now = moved(first, slot, y) * second[0, pl.ds(PAD + y, chunk), :]
            out[0, 0, pl.ds(y, chunk), :] = now
            rounded[pl.ds(y, chunk), :] = now.astype(jnp.bfloat16)

    @pl.when(level != 0)
    def _():
        for y in range(0, ny, chunk):
            now = moved(first, slot, y)
            out[0, 0, pl.ds(y, chunk), :] = now
            rounded[pl.ds(y, chunk), :] = now.astype(jnp.bfloat16)

    projected = lax.dot_general(
        table[...], rounded[...], (((1,), (1,)), ((), ())), preferred_element_type=jnp.float32
    )
    bin_row = bins[pl.ds(column, 1), :]
    half = NBIN * 2 * NW
    dry = jnp.zeros((2 * NW, ny), jnp.float32)
    wet = jnp.zeros((2 * NW, ny), jnp.float32)
    for k in range(NBIN):
        chosen = bin_row == k
        dry = dry + jnp.where(chosen, projected[2 * NW * k : 2 * NW * (k + 1)], 0.0)
        wet = wet + jnp.where(chosen, projected[half + 2 * NW * k : half + 2 * NW * (k + 1)], 0.0)
    moisture = strip[column + SUB, pl.ds(2 * levels + level, 1), :]
    thickness = strip[column + SUB, pl.ds(3 * levels + level, 1), :]
    growth = moisture / (1.0 - moisture)
    opt[0, 0] = (dry + growth * wet) * thickness


def chem_call(edge, extras, shared, earlier):
    tracer, strip, bins, kinds, table, settle = shared
    levels, width, ny, species = tracer.shape
    local = 2 * SUB + 1 if edge else width
    steps = 2 * SUB if edge else width - 2 * SUB
    last = levels - 1

    if edge:
        def place(l, i):
            return (last - l, jnp.where(i < SUB, i, i + width - 2 * SUB), 0, 0)
    else:
        def place(l, i):
            return (last - l, i + SUB, 0, 0)

    def whole(l, i):
        return (last - l, 0, 0, 0)

    halo_spec = pl.BlockSpec((1, SUB, ny, species), whole)
    kept_spec = pl.BlockSpec((1, 8, ny, species), whole)
    in_specs = [pl.BlockSpec((1, width, ny, species), whole)] + [VMEM_SPEC] * 5
    inputs = (tracer,)
    aliases = {}
    if edge:
        far = width // 2 - 1
        in_specs = [SMEM_SPEC, VMEM_SPEC, halo_spec, halo_spec, kept_spec]
        in_specs += [
            pl.BlockSpec((1, 2, ny, species), whole),
            pl.BlockSpec((1, 2, ny, species), lambda l, i: (last - l, far, 0, 0)),
        ]
        in_specs += [VMEM_SPEC] * 5
        inputs = (tracer, tracer)
        in_specs += [pl.BlockSpec(memory_space=pl.ANY)] * 2
        aliases = {len(in_specs) - 2: 0, len(in_specs) - 1: 1}
    cells = levels * local * ny * species
    return pl.pallas_call(
        functools.partial(chem_kernel, levels, width, edge),
        grid=(levels, steps),
        in_specs=in_specs,
        out_specs=[
            pl.BlockSpec((1, 1, ny, species), place),
            pl.BlockSpec((1, 1, 2 * NW, ny), place),
        ]
        + ([] if edge else [kept_spec]),
        out_shape=[
            jax.ShapeDtypeStruct((levels, width, ny, species), jnp.float32),
            jax.ShapeDtypeStruct((levels, width, 2 * NW, ny), jnp.float32),
        ]
        + ([] if edge else [jax.ShapeDtypeStruct((levels, 8, ny, species), jnp.float32)]),
        scratch_shapes=[
            pltpu.VMEM((local, ny + 2 * PAD, species), jnp.float32),
            pltpu.VMEM((local, ny + 2 * PAD, species), jnp.float32),
            pltpu.VMEM((local, ny, species), jnp.float32),
            pltpu.VMEM((local, ny, species), jnp.float32),
            pltpu.VMEM((ny, species), jnp.bfloat16),
        ],
        input_output_aliases=aliases,
        compiler_params=pltpu.CompilerParams(
            dimension_semantics=("arbitrary", "arbitrary"),
            vmem_limit_bytes=60 * 1024 * 1024,
        ),
        cost_estimate=pl.CostEstimate(
            flops=cells * 40, bytes_accessed=cells * 6, transcendentals=0
        ),
        name="edge_columns" if edge else "inner_columns",
    )(*extras, *inputs, strip, bins, kinds, table, settle, *earlier)


def radiate(optical, cosine, sunlight):
    overhead = jnp.zeros_like(optical[0, :, :NW])
    layers = [None] * optical.shape[0]
    for height in reversed(range(optical.shape[0])):
        transmitted = jnp.exp(-overhead / cosine[:, None])
        layers[height] = cosine * jnp.sum(
            sunlight[None, :, None] * optical[height, :, NW:] * transmitted, axis=1
        )
        overhead = overhead + optical[height, :, :NW]
    return jnp.stack(layers, axis=1)


def per_device(
    tracer_amounts,
    zonal_transit_ratio,
    meridional_transit_ratio,
    moisture_ratio,
    stratum_depths,
    sun_elevation_factor,
    thermal_anomaly,
    particle_class_map,
    ground_cover_kind,
    arid_extinction_table,
    swelling_factors,
    settling_velocities,
    arriving_irradiance,
):
    levels, width, ny, species = tracer_amounts.shape
    gx_count = lax.axis_size("gx")
    gy_count = lax.axis_size("gy")
    total = gx_count * gy_count
    gx = lax.axis_index("gx")
    gy = lax.axis_index("gy")
    tile_x, tile_y = sun_elevation_factor.shape
    both = ("gx", "gy")
    fields = jnp.concatenate(
        [zonal_transit_ratio, meridional_transit_ratio, moisture_ratio, stratum_depths], axis=0
    )
    field_count = fields.shape[0]
    fields = jnp.pad(fields.transpose(1, 0, 2), ((SUB, SUB), (0, 0), (0, 0)))
    t = thermal_anomaly
    span_y = max(tile_x, tile_y)

    def edge_rows(rows):
        return jnp.pad(rows, ((0, 8 - levels), (0, span_y - rows.shape[1])))

    fringe = jnp.stack(
        [edge_rows(t[:, 0]), edge_rows(t[:, -1]), edge_rows(t[:, :, 0]), edge_rows(t[:, :, -1])]
    )
    dma = pltpu.SemaphoreType.DMA
    strip, rim, strip_sun, fringe_in = pl.pallas_call(
        functools.partial(fields_kernel, gx_count, gy_count, width),
        in_specs=[VMEM_SPEC] * 3,
        out_specs=[VMEM_SPEC] * 4,
        out_shape=[
            jax.ShapeDtypeStruct((width + 2 * SUB, field_count, ny), jnp.float32),
            jax.ShapeDtypeStruct((2, SUB, field_count, ny), jnp.float32),
            jax.ShapeDtypeStruct((width, ny), jnp.float32),
            jax.ShapeDtypeStruct(fringe.shape, jnp.float32),
        ],
        scratch_shapes=[
            dma((gy_count,)), dma((gy_count,)), dma((gy_count,)), dma((gy_count,)),
            dma((2,)), dma((gy_count,)), dma((4,)), dma((4,)),
        ],
        compiler_params=pltpu.CompilerParams(collective_id=0, has_side_effects=True),
        name="field_exchange",
    )(fields, sun_elevation_factor, fringe)

    tail, head, strip = lax.optimization_barrier(
        (tracer_amounts[:, width - SUB :], tracer_amounts[:, :SUB], strip)
    )
    halo_w = lax.ppermute(tail, both, [(i, i + 1) for i in range(total - 1)])
    halo_e = lax.ppermute(head, both, [(i + 1, i) for i in range(total - 1)])

    east_row = jnp.where(gx == gx_count - 1, 0.0, fringe_in[0, :levels, :tile_y])
    west_row = jnp.where(gx == 0, 0.0, fringe_in[1, :levels, :tile_y])
    north_col = jnp.where(gy == gy_count - 1, 0.0, fringe_in[2, :levels, :tile_x])
    south_col = jnp.where(gy == 0, 0.0, fringe_in[3, :levels, :tile_x])
    wide_x = jnp.concatenate([west_row[:, None], t, east_row[:, None]], axis=1)
    wide_y = jnp.concatenate([south_col[:, :, None], t, north_col[:, :, None]], axis=2)
    laplace = wide_x[:, 2:] + wide_x[:, :-2] + wide_y[:, :, 2:] + wide_y[:, :, :-2] - 4.0 * t
    base = t + SPREAD_FACTOR * laplace

    table = jnp.concatenate([arid_extinction_table, swelling_factors], axis=1).T
    land = jnp.pad(
        settling_velocities, ((0, LAND_ROWS - settling_velocities.shape[0]), (0, 0))
    )
    high = lax.reduce_precision(land, 8, 7)
    middle = lax.reduce_precision(land - high, 8, 7)
    settle = jnp.concatenate([high, middle, land - high - middle], axis=0).astype(jnp.bfloat16)
    shared = (
        tracer_amounts, strip, particle_class_map, ground_cover_kind, table, settle,
    )
    updated, optical, saved = chem_call(False, (), shared, ())
    flags = jnp.stack(
        [gy == 0, (gx > 0) | (gy > 0), gy == gy_count - 1, (gx < gx_count - 1) | (gy < gy_count - 1)]
    ).astype(jnp.int32)
    updated, optical = chem_call(
        True, (flags, rim, halo_w, halo_e, saved), shared, (updated, optical)
    )
    heat = radiate(optical, strip_sun, arriving_irradiance)
    anomaly = pl.pallas_call(
        functools.partial(return_kernel, gx_count, gy_count, width),
        in_specs=[VMEM_SPEC] * 2,
        out_specs=VMEM_SPEC,
        out_shape=jax.ShapeDtypeStruct(t.shape, jnp.float32),
        scratch_shapes=[
            pltpu.VMEM((tile_x, levels, tile_y), jnp.float32),
            dma((gy_count,)), dma((gy_count,)),
        ],
        compiler_params=pltpu.CompilerParams(collective_id=1, has_side_effects=True),
        name="heat_return",
    )(heat, base)
    return (updated, anomaly)


def solution(mesh):
    return jax.shard_map(
        per_device,
        mesh=mesh,
        in_specs=(
            P(None, ("gx", "gy"), None, None),
            P(None, "gx", "gy"),
            P(None, "gx", "gy"),
            P(None, "gx", "gy"),
            P(None, "gx", "gy"),
            P("gx", "gy"),
            P(None, "gx", "gy"),
            P(("gx", "gy"), None),
            P(("gx", "gy"), None),
            P(),
            P(),
            P(),
            P(),
        ),
        out_specs=(P(None, ("gx", "gy"), None, None), P(None, "gx", "gy")),
        check_vma=False,
    )
```

```python
import functools

import jax
import jax.numpy as jnp
from jax import lax
from jax.experimental import pallas as pl
from jax.experimental.pallas import tpu as pltpu
from jax.sharding import PartitionSpec as P

SUB = 3
NBIN = 8
NW = 4
SPREAD_FACTOR = 0.2
PAD = 8
LAND_ROWS = 32
MESH = pl.DeviceIdType.MESH
VMEM_SPEC = pl.BlockSpec(memory_space=pltpu.VMEM)
SMEM_SPEC = pl.BlockSpec(memory_space=pltpu.SMEM)


def greet(gx_count, gy_count, reach):
    gx = lax.axis_index("gx")
    gy = lax.axis_index("gy")
    barrier = pltpu.get_barrier_semaphore()
    for dx in range(-reach, reach + 1):
        for dy in range(gy_count):
            if dx == 0 and dy == 0:
                continue
            pl.semaphore_signal(
                barrier,
                inc=1,
                device_id=(
                    lax.rem(gx + dx + gx_count, gx_count),
                    lax.rem(gy + dy, gy_count),
                ),
                device_id_type=MESH,
            )
    pl.semaphore_wait(barrier, (2 * reach + 1) * gy_count - 1)


def fields_kernel(
    gx_count, gy_count, width,
    zonal, merid, moisture, depth, sun, fringe,
    strip, rim, strip_sun, fringe_in, fields,
    send_a, recv_a, send_s, recv_s, send_r, recv_r, send_f, recv_f,
):
    gx = lax.axis_index("gx")
    gy = lax.axis_index("gy")
    span = width + 2 * SUB
    tile_x = width * gy_count
    tile_y = fields.shape[2]
    right = lax.rem(gx + 1, gx_count)
    left = lax.rem(gx + gx_count - 1, gx_count)
    up = lax.rem(gy + 1, gy_count)
    down = lax.rem(gy + gy_count - 1, gy_count)
    margin = jnp.zeros((SUB,) + fields.shape[1:], jnp.float32)
    fields[pl.ds(0, SUB)] = margin
    fields[pl.ds(SUB + tile_x, SUB)] = margin
    levels = zonal.shape[0]
    for k, field in enumerate((zonal, merid, moisture, depth)):
        for level in range(levels):
            fields[pl.ds(SUB, tile_x), k * levels + level, :] = field[level]
    greet(gx_count, gy_count, 1)
    mine = pl.ds(pl.multiple_of(gy * tile_y, tile_y), tile_y)

    def rims(side):
        lo = tile_x if side == 0 else SUB
        return pltpu.make_async_remote_copy(
            src_ref=fields.at[pl.ds(lo, SUB)],
            dst_ref=rim.at[side, :, :, mine],
            send_sem=send_r.at[side],
            recv_sem=recv_r.at[gy],
            device_id=((right, 0) if side == 0 else (left, gy_count - 1)),
            device_id_type=MESH,
        )

    def slab(peer):
        return pltpu.make_async_remote_copy(
            src_ref=fields.at[pl.ds(peer * width, span)],
            dst_ref=strip.at[:, :, mine],
            send_sem=send_a.at[peer],
            recv_sem=recv_a.at[gy],
            device_id=(gx, peer),
            device_id_type=MESH,
        )

    def sunny(peer):
        return pltpu.make_async_remote_copy(
            src_ref=sun.at[pl.ds(peer * width, width)],
            dst_ref=strip_sun.at[:, mine],
            send_sem=send_s.at[peer],
            recv_sem=recv_s.at[gy],
            device_id=(gx, peer),
            device_id_type=MESH,
        )

    targets = ((left, gy), (right, gy), (gx, down), (gx, up))
    edges = [
        pltpu.make_async_remote_copy(
            src_ref=fringe.at[k],
            dst_ref=fringe_in.at[k],
            send_sem=send_f.at[k],
            recv_sem=recv_f.at[k],
            device_id=targets[k],
            device_id_type=MESH,
        )
        for k in range(4)
    ]
    for peer in range(gy_count):
        @pl.when(gy != peer)
        def _(peer=peer):
            slab(peer).start()
            sunny(peer).start()
    for side in range(2):
        rims(side).start()
    for edge in edges:
        edge.start()
    strip[:, :, mine] = fields[pl.ds(gy * width, span)]
    strip_sun[:, mine] = sun[pl.ds(pl.multiple_of(gy * width, width), width), :]
    for edge in edges:
        edge.wait()
    for side in range(2):
        rims(side).wait_send()
    for peer in range(gy_count):
        @pl.when(gy != peer)
        def _(peer=peer):
            slab(peer).wait_send()
            sunny(peer).wait_send()
            theirs = pl.ds(peer * tile_y, tile_y)
            pltpu.make_async_remote_copy(
                src_ref=fields.at[pl.ds(0, span)],
                dst_ref=strip.at[:, :, theirs],
                send_sem=send_a.at[peer],
                recv_sem=recv_a.at[peer],
                device_id=(gx, peer),
                device_id_type=MESH,
            ).wait_recv()
            pltpu.make_async_remote_copy(
                src_ref=sun.at[pl.ds(0, width)],
                dst_ref=strip_sun.at[:, theirs],
                send_sem=send_s.at[peer],
                recv_sem=recv_s.at[peer],
                device_id=(gx, peer),
                device_id_type=MESH,
            ).wait_recv()
    for side, owner, source in ((0, 0, left), (1, gy_count - 1, right)):
        @pl.when(gy == owner)
        def _(side=side, source=source):
            for peer in range(gy_count):
                pltpu.make_async_remote_copy(
                    src_ref=fields.at[pl.ds(0, SUB)],
                    dst_ref=rim.at[side, :, :, pl.ds(peer * tile_y, tile_y)],
                    send_sem=send_r.at[side],
                    recv_sem=recv_r.at[peer],
                    device_id=(source, peer),
                    device_id_type=MESH,
                ).wait_recv()


def return_kernel(
    gx_count, gy_count, width,
    optical, sun, light, base, out, heat, tile, send_sem, recv_sem,
):
    gx = lax.axis_index("gx")
    gy = lax.axis_index("gy")
    tile_y = base.shape[2]

    def radiate(x, carry):
        cosine = sun[pl.ds(x, 1), :]
        inverse = 1.0 / cosine
        overhead = [jnp.zeros_like(cosine) for _ in range(NW)]
        for level in reversed(range(optical.shape[0])):
            warmth = jnp.zeros_like(cosine)
            for w in range(NW):
                transmitted = jnp.exp(-overhead[w] * inverse)
                absorbed = optical[level, x, pl.ds(NW + w, 1), :]
                warmth = warmth + light[w] * absorbed * transmitted
                overhead[w] = overhead[w] + optical[level, x, pl.ds(w, 1), :]
            heat[x, pl.ds(level, 1), :] = cosine * warmth
        return carry

    lax.fori_loop(0, width, radiate, 0)
    greet(gx_count, gy_count, 0)

    def slab(peer):
        return pltpu.make_async_remote_copy(
            src_ref=heat.at[:, :, pl.ds(peer * tile_y, tile_y)],
            dst_ref=tile.at[pl.ds(gy * width, width)],
            send_sem=send_sem.at[peer],
            recv_sem=recv_sem.at[gy],
            device_id=(gx, peer),
            device_id_type=MESH,
        )

    for peer in range(gy_count):
        @pl.when(gy != peer)
        def _(peer=peer):
            slab(peer).start()
    mine = pl.ds(pl.multiple_of(gy * tile_y, tile_y), tile_y)
    tile[pl.ds(gy * width, width)] = heat[:, :, mine]
    for peer in range(gy_count):
        @pl.when(gy != peer)
        def _(peer=peer):
            slab(peer).wait_send()
            pltpu.make_async_remote_copy(
                src_ref=heat.at[:, :, pl.ds(0, tile_y)],
                dst_ref=tile.at[pl.ds(peer * width, width)],
                send_sem=send_sem.at[peer],
                recv_sem=recv_sem.at[peer],
                device_id=(gx, peer),
                device_id_type=MESH,
            ).wait_recv()
    for level in range(base.shape[0]):
        out[level] = base[level] + tile[:, level, :]


def tn_dot(left, right):
    return lax.dot_general(
        left, right, (((0,), (0,)), ((), ())), preferred_element_type=jnp.float32
    )


def three_parts(rows):
    high = rows.astype(jnp.bfloat16).astype(jnp.float32)
    rest = rows - high
    middle = rest.astype(jnp.bfloat16).astype(jnp.float32)
    return jnp.concatenate([high, middle, rest - middle], axis=0).astype(jnp.bfloat16)


def chem_kernel(levels, width, edge, *refs):
    if edge:
        (flags, rim, halo_w, halo_e, saved, near_w, near_e, strip, bins, kinds, table, settle,
         _out_in, _opt_in, out, opt, first, second, zonal, merid, rounded) = refs
    else:
        (tracer, strip, bins, kinds, table, settle,
         out, opt, saved, first, second, zonal, merid, rounded) = refs
    level = levels - 1 - pl.program_id(0)
    step = pl.program_id(1)
    ny = strip.shape[2]
    fields = strip.shape[1]
    local = first.shape[0]
    chunk = 64

    def selector(row):
        which = lax.rem(lax.broadcasted_iota(jnp.int32, (3 * fields, 128), 0), fields)
        return jnp.where(which == row, 1.0, 0.0).astype(jnp.bfloat16)

    def coefficients(slot, rows):
        parts = three_parts(rows)
        zonal[slot] = tn_dot(parts, selector(level))
        merid[slot] = tn_dot(parts, selector(levels + level))

    def moved(source, slot, y):
        here = source[slot, pl.ds(PAD + y, chunk), :]
        c = zonal[slot, pl.ds(y, chunk), :]
        d = merid[slot, pl.ds(y, chunk), :]
        across = jnp.where(
            c > 0.0,
            source[slot - 1, pl.ds(PAD + y, chunk), :],
            source[slot + 1, pl.ds(PAD + y, chunk), :],
        )
        along = jnp.where(
            d > 0.0,
            source[slot, pl.ds(PAD - 1 + y, chunk), :],
            source[slot, pl.ds(PAD + 1 + y, chunk), :],
        )
        return here + jnp.abs(c) * (across - here) + jnp.abs(d) * (along - here)

    def advance(source, target, low, high):
        def column(slot, carry):
            for y in range(0, ny, chunk):
                target[slot, pl.ds(PAD + y, chunk), :] = moved(source, slot, y)
            return carry

        lax.fori_loop(low, high, column, 0)

    @pl.when((pl.program_id(0) == 0) & (step == 0))
    def _():
        zeros = jnp.zeros((local, PAD, 128), jnp.float32)
        for buffer in (first, second):
            buffer[:, pl.ds(0, PAD), :] = zeros
            buffer[:, pl.ds(PAD + ny, PAD), :] = zeros

    body = pl.ds(PAD, ny)
    if edge:
        @pl.when(step == 0)
        def _():
            for j in (1, 2):
                rows = jnp.where(flags[0] == 1, rim[0, j], strip[j])
                coefficients(j, jnp.where(flags[1] == 1, rows, 0.0))
            for j in (3, 4, 5):
                coefficients(j, strip[j])
            for j in range(SUB):
                first[j, body, :] = halo_w[0, j].astype(jnp.float32)
            for j in range(2):
                first[SUB + j, body, :] = near_w[0, j].astype(jnp.float32)
                second[SUB + 1 + j, body, :] = saved[0, j]
            advance(first, second, 1, 4)
            advance(second, first, 2, 5)
            for j in range(2):
                first[SUB + 2 + j, body, :] = saved[0, 2 + j]

        @pl.when(step == SUB)
        def _():
            for j in (1, 2, 3):
                coefficients(j, strip[width - 1 + j])
            for j in (4, 5):
                rows = jnp.where(flags[2] == 1, rim[1, j - 4], strip[width - 1 + j])
                coefficients(j, jnp.where(flags[3] == 1, rows, 0.0))
            for j in range(SUB):
                first[4 + j, body, :] = halo_e[0, j].astype(jnp.float32)
            for j in range(2):
                first[2 + j, body, :] = near_e[0, j].astype(jnp.float32)
                second[1 + j, body, :] = saved[0, 4 + j]
            advance(first, second, 3, 6)
            advance(second, first, 2, 5)
            for j in range(2):
                first[j, body, :] = saved[0, 6 + j]

        slot = jnp.where(step < SUB, step + SUB, step - 2)
        column = jnp.where(step < SUB, step, step + width - 2 * SUB)
    else:
        @pl.when(step == 0)
        def _():
            def load(j, carry):
                coefficients(j, strip[j + SUB])
                first[j, body, :] = tracer[0, j].astype(jnp.float32)
                return carry

            lax.fori_loop(0, local, load, 0)
            advance(first, second, 1, local - 1)
            advance(second, first, 2, local - 2)
            kept = (
                (second, 1), (second, 2), (first, 2), (first, 3),
                (second, local - 3), (second, local - 2), (first, local - 4), (first, local - 3),
            )
            for k, (buffer, place) in enumerate(kept):
                saved[0, k] = buffer[place, body, :]

        slot = SUB + step
        column = slot

    kind_row = kinds[pl.ds(column, 1), :]
    rows_here = strip[column + SUB]

    @pl.when(level == 0)
    def _():
        which = lax.rem(lax.broadcasted_iota(jnp.int32, (3 * LAND_ROWS, ny), 0), LAND_ROWS)
        one_hot = jnp.where(which == kind_row, 1.0, 0.0).astype(jnp.bfloat16)
        speed = tn_dot(one_hot, settle[...])
        depth = tn_dot(three_parts(rows_here), selector(3 * levels))
        second[0, body, :] = depth / (depth + speed)

    @pl.when(level == 0)
    def _():
        for y in range(0, ny, chunk):
            now = moved(first, slot, y) * second[0, pl.ds(PAD + y, chunk), :]
            out[0, 0, pl.ds(y, chunk), :] = now
            rounded[pl.ds(y, chunk), :] = now.astype(jnp.bfloat16)

    @pl.when(level != 0)
    def _():
        for y in range(0, ny, chunk):
            now = moved(first, slot, y)
            out[0, 0, pl.ds(y, chunk), :] = now
            rounded[pl.ds(y, chunk), :] = now.astype(jnp.bfloat16)

    projected = lax.dot_general(
        table[...], rounded[...], (((1,), (1,)), ((), ())), preferred_element_type=jnp.float32
    )
    bin_row = bins[pl.ds(column, 1), :]
    half = NBIN * 2 * NW
    dry = jnp.zeros((2 * NW, ny), jnp.float32)
    wet = jnp.zeros((2 * NW, ny), jnp.float32)
    for k in range(NBIN):
        chosen = bin_row == k
        dry = dry + jnp.where(chosen, projected[2 * NW * k : 2 * NW * (k + 1)], 0.0)
        wet = wet + jnp.where(chosen, projected[half + 2 * NW * k : half + 2 * NW * (k + 1)], 0.0)
    moisture = strip[column + SUB, pl.ds(2 * levels + level, 1), :]
    thickness = strip[column + SUB, pl.ds(3 * levels + level, 1), :]
    growth = moisture / (1.0 - moisture)
    opt[0, 0] = (dry + growth * wet) * thickness


def chem_call(edge, extras, shared, earlier):
    tracer, strip, bins, kinds, table, settle = shared
    levels, width, ny, species = tracer.shape
    local = 2 * SUB + 1 if edge else width
    steps = 2 * SUB if edge else width - 2 * SUB
    last = levels - 1

    if edge:
        def place(l, i):
            return (last - l, jnp.where(i < SUB, i, i + width - 2 * SUB), 0, 0)
    else:
        def place(l, i):
            return (last - l, i + SUB, 0, 0)

    def whole(l, i):
        return (last - l, 0, 0, 0)

    halo_spec = pl.BlockSpec((1, SUB, ny, species), whole)
    kept_spec = pl.BlockSpec((1, 8, ny, species), whole)
    in_specs = [pl.BlockSpec((1, width, ny, species), whole)] + [VMEM_SPEC] * 5
    inputs = (tracer,)
    aliases = {}
    if edge:
        far = width // 2 - 1
        in_specs = [SMEM_SPEC, VMEM_SPEC, halo_spec, halo_spec, kept_spec]
        in_specs += [
            pl.BlockSpec((1, 2, ny, species), whole),
            pl.BlockSpec((1, 2, ny, species), lambda l, i: (last - l, far, 0, 0)),
        ]
        in_specs += [VMEM_SPEC] * 5
        inputs = (tracer, tracer)
        in_specs += [pl.BlockSpec(memory_space=pl.ANY)] * 2
        aliases = {len(in_specs) - 2: 0, len(in_specs) - 1: 1}
    cells = levels * local * ny * species
    return pl.pallas_call(
        functools.partial(chem_kernel, levels, width, edge),
        grid=(levels, steps),
        in_specs=in_specs,
        out_specs=[
            pl.BlockSpec((1, 1, ny, species), place),
            pl.BlockSpec((1, 1, 2 * NW, ny), place),
        ]
        + ([] if edge else [kept_spec]),
        out_shape=[
            jax.ShapeDtypeStruct((levels, width, ny, species), jnp.float32),
            jax.ShapeDtypeStruct((levels, width, 2 * NW, ny), jnp.float32),
        ]
        + ([] if edge else [jax.ShapeDtypeStruct((levels, 8, ny, species), jnp.float32)]),
        scratch_shapes=[
            pltpu.VMEM((local, ny + 2 * PAD, species), jnp.float32),
            pltpu.VMEM((local, ny + 2 * PAD, species), jnp.float32),
            pltpu.VMEM((local, ny, species), jnp.float32),
            pltpu.VMEM((local, ny, species), jnp.float32),
            pltpu.VMEM((ny, species), jnp.bfloat16),
        ],
        input_output_aliases=aliases,
        compiler_params=pltpu.CompilerParams(
            dimension_semantics=("arbitrary", "arbitrary"),
            vmem_limit_bytes=60 * 1024 * 1024,
        ),
        cost_estimate=pl.CostEstimate(
            flops=cells * 40, bytes_accessed=cells * 6, transcendentals=0
        ),
        name="edge_columns" if edge else "inner_columns",
    )(*extras, *inputs, strip, bins, kinds, table, settle, *earlier)


def per_device(
    tracer_amounts,
    zonal_transit_ratio,
    meridional_transit_ratio,
    moisture_ratio,
    stratum_depths,
    sun_elevation_factor,
    thermal_anomaly,
    particle_class_map,
    ground_cover_kind,
    arid_extinction_table,
    swelling_factors,
    settling_velocities,
    arriving_irradiance,
):
    levels, width, ny, species = tracer_amounts.shape
    gx_count = lax.axis_size("gx")
    gy_count = lax.axis_size("gy")
    total = gx_count * gy_count
    gx = lax.axis_index("gx")
    gy = lax.axis_index("gy")
    tile_x, tile_y = sun_elevation_factor.shape
    both = ("gx", "gy")
    field_count = 4 * levels
    t = thermal_anomaly
    span_y = max(tile_x, tile_y)

    def edge_rows(rows):
        return jnp.pad(rows, ((0, 8 - levels), (0, span_y - rows.shape[1])))

    fringe = jnp.stack(
        [edge_rows(t[:, 0]), edge_rows(t[:, -1]), edge_rows(t[:, :, 0]), edge_rows(t[:, :, -1])]
    )
    dma = pltpu.SemaphoreType.DMA
    strip, rim, strip_sun, fringe_in = pl.pallas_call(
        functools.partial(fields_kernel, gx_count, gy_count, width),
        in_specs=[VMEM_SPEC] * 6,
        out_specs=[VMEM_SPEC] * 4,
        out_shape=[
            jax.ShapeDtypeStruct((width + 2 * SUB, field_count, ny), jnp.float32),
            jax.ShapeDtypeStruct((2, SUB, field_count, ny), jnp.float32),
            jax.ShapeDtypeStruct((width, ny), jnp.float32),
            jax.ShapeDtypeStruct(fringe.shape, jnp.float32),
        ],
        scratch_shapes=[
            pltpu.VMEM((tile_x + 2 * SUB, field_count, tile_y), jnp.float32),
            dma((gy_count,)), dma((gy_count,)), dma((gy_count,)), dma((gy_count,)),
            dma((2,)), dma((gy_count,)), dma((4,)), dma((4,)),
        ],
        compiler_params=pltpu.CompilerParams(collective_id=0, has_side_effects=True),
        name="field_exchange",
    )(
        zonal_transit_ratio, meridional_transit_ratio, moisture_ratio, stratum_depths,
        sun_elevation_factor, fringe,
    )

    tail, head, strip = lax.optimization_barrier(
        (tracer_amounts[:, width - SUB :], tracer_amounts[:, :SUB], strip)
    )
    halo_w = lax.ppermute(tail, both, [(i, i + 1) for i in range(total - 1)])
    halo_e = lax.ppermute(head, both, [(i + 1, i) for i in range(total - 1)])

    east_row = jnp.where(gx == gx_count - 1, 0.0, fringe_in[0, :levels, :tile_y])
    west_row = jnp.where(gx == 0, 0.0, fringe_in[1, :levels, :tile_y])
    north_col = jnp.where(gy == gy_count - 1, 0.0, fringe_in[2, :levels, :tile_x])
    south_col = jnp.where(gy == 0, 0.0, fringe_in[3, :levels, :tile_x])
    wide_x = jnp.concatenate([west_row[:, None], t, east_row[:, None]], axis=1)
    wide_y = jnp.concatenate([south_col[:, :, None], t, north_col[:, :, None]], axis=2)
    laplace = wide_x[:, 2:] + wide_x[:, :-2] + wide_y[:, :, 2:] + wide_y[:, :, :-2] - 4.0 * t
    base = t + SPREAD_FACTOR * laplace

    table = jnp.concatenate([arid_extinction_table, swelling_factors], axis=1).T
    land = jnp.pad(
        settling_velocities, ((0, LAND_ROWS - settling_velocities.shape[0]), (0, 0))
    )
    high = lax.reduce_precision(land, 8, 7)
    middle = lax.reduce_precision(land - high, 8, 7)
    settle = jnp.concatenate([high, middle, land - high - middle], axis=0).astype(jnp.bfloat16)
    shared = (
        tracer_amounts, strip, particle_class_map, ground_cover_kind, table, settle,
    )
    updated, optical, saved = chem_call(False, (), shared, ())
    flags = jnp.stack(
        [gy == 0, (gx > 0) | (gy > 0), gy == gy_count - 1, (gx < gx_count - 1) | (gy < gy_count - 1)]
    ).astype(jnp.int32)
    updated, optical = chem_call(
        True, (flags, rim, halo_w, halo_e, saved), shared, (updated, optical)
    )
    anomaly = pl.pallas_call(
        functools.partial(return_kernel, gx_count, gy_count, width),
        in_specs=[VMEM_SPEC, VMEM_SPEC, SMEM_SPEC, VMEM_SPEC],
        out_specs=VMEM_SPEC,
        out_shape=jax.ShapeDtypeStruct(t.shape, jnp.float32),
        scratch_shapes=[
            pltpu.VMEM((width, levels, ny), jnp.float32),
            pltpu.VMEM((tile_x, levels, tile_y), jnp.float32),
            dma((gy_count,)), dma((gy_count,)),
        ],
        compiler_params=pltpu.CompilerParams(collective_id=1, has_side_effects=True),
        name="heat_return",
    )(optical, strip_sun, arriving_irradiance, base)
    return (updated, anomaly)


def solution(mesh):
    return jax.shard_map(
        per_device,
        mesh=mesh,
        in_specs=(
            P(None, ("gx", "gy"), None, None),
            P(None, "gx", "gy"),
            P(None, "gx", "gy"),
            P(None, "gx", "gy"),
            P(None, "gx", "gy"),
            P("gx", "gy"),
            P(None, "gx", "gy"),
            P(("gx", "gy"), None),
            P(("gx", "gy"), None),
            P(),
            P(),
            P(),
            P(),
        ),
        out_specs=(P(None, ("gx", "gy"), None, None), P(None, "gx", "gy")),
        check_vma=False,
    )
```

```python
import functools

import jax
import jax.numpy as jnp
from jax import lax
from jax.experimental import pallas as pl
from jax.experimental.pallas import tpu as pltpu
from jax.sharding import PartitionSpec as P

SUB = 3
NBIN = 8
NW = 4
SPREAD_FACTOR = 0.2
PAD = 8
LAND_ROWS = 32
MESH = pl.DeviceIdType.MESH
VMEM_SPEC = pl.BlockSpec(memory_space=pltpu.VMEM)
SMEM_SPEC = pl.BlockSpec(memory_space=pltpu.SMEM)


def greet(gx_count, gy_count, reach):
    gx = lax.axis_index("gx")
    gy = lax.axis_index("gy")
    barrier = pltpu.get_barrier_semaphore()
    for dx in range(-reach, reach + 1):
        for dy in range(gy_count):
            if dx == 0 and dy == 0:
                continue
            pl.semaphore_signal(
                barrier,
                inc=1,
                device_id=(
                    lax.rem(gx + dx + gx_count, gx_count),
                    lax.rem(gy + dy, gy_count),
                ),
                device_id_type=MESH,
            )
    pl.semaphore_wait(barrier, (2 * reach + 1) * gy_count - 1)


def fields_kernel(
    gx_count, gy_count, width,
    zonal, merid, moisture, depth, sun, fringe,
    strip, rim, strip_sun, fringe_in, fields, landed,
    send_a, recv_a, send_s, recv_s, send_r, recv_r, send_f, recv_f,
):
    gx = lax.axis_index("gx")
    gy = lax.axis_index("gy")
    span = width + 2 * SUB
    tile_x = width * gy_count
    tile_y = fields.shape[2]
    right = lax.rem(gx + 1, gx_count)
    left = lax.rem(gx + gx_count - 1, gx_count)
    up = lax.rem(gy + 1, gy_count)
    down = lax.rem(gy + gy_count - 1, gy_count)
    margin = jnp.zeros((SUB,) + fields.shape[1:], jnp.float32)
    fields[pl.ds(0, SUB)] = margin
    fields[pl.ds(SUB + tile_x, SUB)] = margin
    levels = zonal.shape[0]
    for k, field in enumerate((zonal, merid, moisture, depth)):
        for level in range(levels):
            fields[pl.ds(SUB, tile_x), k * levels + level, :] = field[level]
    greet(gx_count, gy_count, 1)
    mine = pl.ds(pl.multiple_of(gy * tile_y, tile_y), tile_y)

    def rims(side):
        lo = tile_x if side == 0 else SUB
        return pltpu.make_async_remote_copy(
            src_ref=fields.at[pl.ds(lo, SUB)],
            dst_ref=rim.at[side, :, :, mine],
            send_sem=send_r.at[side],
            recv_sem=recv_r.at[gy],
            device_id=((right, 0) if side == 0 else (left, gy_count - 1)),
            device_id_type=MESH,
        )

    def slab(peer):
        return pltpu.make_async_remote_copy(
            src_ref=fields.at[pl.ds(peer * width, span)],
            dst_ref=landed.at[gy],
            send_sem=send_a.at[peer],
            recv_sem=recv_a.at[gy],
            device_id=(gx, peer),
            device_id_type=MESH,
        )

    def sunny(peer):
        return pltpu.make_async_remote_copy(
            src_ref=sun.at[pl.ds(peer * width, width)],
            dst_ref=strip_sun.at[:, mine],
            send_sem=send_s.at[peer],
            recv_sem=recv_s.at[gy],
            device_id=(gx, peer),
            device_id_type=MESH,
        )

    targets = ((left, gy), (right, gy), (gx, down), (gx, up))
    edges = [
        pltpu.make_async_remote_copy(
            src_ref=fringe.at[k],
            dst_ref=fringe_in.at[k],
            send_sem=send_f.at[k],
            recv_sem=recv_f.at[k],
            device_id=targets[k],
            device_id_type=MESH,
        )
        for k in range(4)
    ]
    for peer in range(gy_count):
        @pl.when(gy != peer)
        def _(peer=peer):
            slab(peer).start()
            sunny(peer).start()
    for side in range(2):
        rims(side).start()
    for edge in edges:
        edge.start()
    strip[:, :, mine] = fields[pl.ds(gy * width, span)]
    strip_sun[:, mine] = sun[pl.ds(pl.multiple_of(gy * width, width), width), :]
    for edge in edges:
        edge.wait()
    for side in range(2):
        rims(side).wait_send()
    for peer in range(gy_count):
        @pl.when(gy != peer)
        def _(peer=peer):
            slab(peer).wait_send()
            sunny(peer).wait_send()
            theirs = pl.ds(peer * tile_y, tile_y)
            pltpu.make_async_remote_copy(
                src_ref=fields.at[pl.ds(0, span)],
                dst_ref=landed.at[peer],
                send_sem=send_a.at[peer],
                recv_sem=recv_a.at[peer],
                device_id=(gx, peer),
                device_id_type=MESH,
            ).wait_recv()
            pltpu.make_async_remote_copy(
                src_ref=sun.at[pl.ds(0, width)],
                dst_ref=strip_sun.at[:, theirs],
                send_sem=send_s.at[peer],
                recv_sem=recv_s.at[peer],
                device_id=(gx, peer),
                device_id_type=MESH,
            ).wait_recv()
            strip[:, :, theirs] = landed[peer]
    for side, owner, source in ((0, 0, left), (1, gy_count - 1, right)):
        @pl.when(gy == owner)
        def _(side=side, source=source):
            for peer in range(gy_count):
                pltpu.make_async_remote_copy(
                    src_ref=fields.at[pl.ds(0, SUB)],
                    dst_ref=rim.at[side, :, :, pl.ds(peer * tile_y, tile_y)],
                    send_sem=send_r.at[side],
                    recv_sem=recv_r.at[peer],
                    device_id=(source, peer),
                    device_id_type=MESH,
                ).wait_recv()


def return_kernel(
    gx_count, gy_count, width,
    optical, sun, light, base, out, heat, tile, send_sem, recv_sem,
):
    gx = lax.axis_index("gx")
    gy = lax.axis_index("gy")
    tile_y = base.shape[2]

    def radiate(x, carry):
        cosine = sun[pl.ds(x, 1), :]
        inverse = 1.0 / cosine
        overhead = [jnp.zeros_like(cosine) for _ in range(NW)]
        for level in reversed(range(optical.shape[0])):
            warmth = jnp.zeros_like(cosine)
            for w in range(NW):
                transmitted = jnp.exp(-overhead[w] * inverse)
                absorbed = optical[level, x, pl.ds(NW + w, 1), :]
                warmth = warmth + light[w] * absorbed * transmitted
                overhead[w] = overhead[w] + optical[level, x, pl.ds(w, 1), :]
            warmth = cosine * warmth
            for peer in range(gy_count):
                heat[peer, x, pl.ds(level, 1), :] = warmth[:, peer * tile_y : (peer + 1) * tile_y]
        return carry

    lax.fori_loop(0, width, radiate, 0)
    greet(gx_count, gy_count, 0)

    def slab(peer):
        return pltpu.make_async_remote_copy(
            src_ref=heat.at[peer],
            dst_ref=tile.at[pl.ds(gy * width, width)],
            send_sem=send_sem.at[peer],
            recv_sem=recv_sem.at[gy],
            device_id=(gx, peer),
            device_id_type=MESH,
        )

    for peer in range(gy_count):
        @pl.when(gy != peer)
        def _(peer=peer):
            slab(peer).start()
    tile[pl.ds(gy * width, width)] = heat[gy]
    for peer in range(gy_count):
        @pl.when(gy != peer)
        def _(peer=peer):
            slab(peer).wait_send()
            pltpu.make_async_remote_copy(
                src_ref=heat.at[peer],
                dst_ref=tile.at[pl.ds(peer * width, width)],
                send_sem=send_sem.at[peer],
                recv_sem=recv_sem.at[peer],
                device_id=(gx, peer),
                device_id_type=MESH,
            ).wait_recv()
    for level in range(base.shape[0]):
        out[level] = base[level] + tile[:, level, :]


def tn_dot(left, right):
    return lax.dot_general(
        left, right, (((0,), (0,)), ((), ())), preferred_element_type=jnp.float32
    )


def three_parts(rows):
    high = rows.astype(jnp.bfloat16).astype(jnp.float32)
    rest = rows - high
    middle = rest.astype(jnp.bfloat16).astype(jnp.float32)
    return jnp.concatenate([high, middle, rest - middle], axis=0).astype(jnp.bfloat16)


def chem_kernel(levels, width, edge, *refs):
    if edge:
        (flags, rim, halo_w, halo_e, saved, near_w, near_e, strip, bins, kinds, table, settle,
         _out_in, _opt_in, out, opt, first, second, zonal, merid, rounded) = refs
    else:
        (tracer, strip, bins, kinds, table, settle,
         out, opt, saved, first, second, zonal, merid, rounded) = refs
    level = levels - 1 - pl.program_id(0)
    step = pl.program_id(1)
    ny = strip.shape[2]
    fields = strip.shape[1]
    local = first.shape[0]
    chunk = 64

    def selector(row):
        which = lax.rem(lax.broadcasted_iota(jnp.int32, (3 * fields, 128), 0), fields)
        return jnp.where(which == row, 1.0, 0.0).astype(jnp.bfloat16)

    def coefficients(slot, rows):
        parts = three_parts(rows)
        zonal[slot] = tn_dot(parts, selector(level))
        merid[slot] = tn_dot(parts, selector(levels + level))

    def moved(source, slot, y):
        here = source[slot, pl.ds(PAD + y, chunk), :]
        c = zonal[slot, pl.ds(y, chunk), :]
        d = merid[slot, pl.ds(y, chunk), :]
        across = jnp.where(
            c > 0.0,
            source[slot - 1, pl.ds(PAD + y, chunk), :],
            source[slot + 1, pl.ds(PAD + y, chunk), :],
        )
        along = jnp.where(
            d > 0.0,
            source[slot, pl.ds(PAD - 1 + y, chunk), :],
            source[slot, pl.ds(PAD + 1 + y, chunk), :],
        )
        return here + jnp.abs(c) * (across - here) + jnp.abs(d) * (along - here)

    def advance(source, target, low, high):
        def column(slot, carry):
            for y in range(0, ny, chunk):
                target[slot, pl.ds(PAD + y, chunk), :] = moved(source, slot, y)
            return carry

        lax.fori_loop(low, high, column, 0)

    @pl.when((pl.program_id(0) == 0) & (step == 0))
    def _():
        zeros = jnp.zeros((local, PAD, 128), jnp.float32)
        for buffer in (first, second):
            buffer[:, pl.ds(0, PAD), :] = zeros
            buffer[:, pl.ds(PAD + ny, PAD), :] = zeros

    body = pl.ds(PAD, ny)
    if edge:
        @pl.when(step == 0)
        def _():
            for j in (1, 2):
                rows = jnp.where(flags[0] == 1, rim[0, j], strip[j])
                coefficients(j, jnp.where(flags[1] == 1, rows, 0.0))
            for j in (3, 4, 5):
                coefficients(j, strip[j])
            for j in range(SUB):
                first[j, body, :] = halo_w[0, j].astype(jnp.float32)
            for j in range(2):
                first[SUB + j, body, :] = near_w[0, j].astype(jnp.float32)
                second[SUB + 1 + j, body, :] = saved[0, j]
            advance(first, second, 1, 4)
            advance(second, first, 2, 5)
            for j in range(2):
                first[SUB + 2 + j, body, :] = saved[0, 2 + j]

        @pl.when(step == SUB)
        def _():
            for j in (1, 2, 3):
                coefficients(j, strip[width - 1 + j])
            for j in (4, 5):
                rows = jnp.where(flags[2] == 1, rim[1, j - 4], strip[width - 1 + j])
                coefficients(j, jnp.where(flags[3] == 1, rows, 0.0))
            for j in range(SUB):
                first[4 + j, body, :] = halo_e[0, j].astype(jnp.float32)
            for j in range(2):
                first[2 + j, body, :] = near_e[0, j].astype(jnp.float32)
                second[1 + j, body, :] = saved[0, 4 + j]
            advance(first, second, 3, 6)
            advance(second, first, 2, 5)
            for j in range(2):
                first[j, body, :] = saved[0, 6 + j]

        slot = jnp.where(step < SUB, step + SUB, step - 2)
        column = jnp.where(step < SUB, step, step + width - 2 * SUB)
    else:
        @pl.when(step == 0)
        def _():
            def load(j, carry):
                coefficients(j, strip[j + SUB])
                first[j, body, :] = tracer[0, j].astype(jnp.float32)
                return carry

            lax.fori_loop(0, local, load, 0)
            advance(first, second, 1, local - 1)
            advance(second, first, 2, local - 2)
            kept = (
                (second, 1), (second, 2), (first, 2), (first, 3),
                (second, local - 3), (second, local - 2), (first, local - 4), (first, local - 3),
            )
            for k, (buffer, place) in enumerate(kept):
                saved[0, k] = buffer[place, body, :]

        slot = SUB + step
        column = slot

    kind_row = kinds[pl.ds(column, 1), :]
    rows_here = strip[column + SUB]

    @pl.when(level == 0)
    def _():
        which = lax.rem(lax.broadcasted_iota(jnp.int32, (3 * LAND_ROWS, ny), 0), LAND_ROWS)
        one_hot = jnp.where(which == kind_row, 1.0, 0.0).astype(jnp.bfloat16)
        speed = tn_dot(one_hot, settle[...])
        depth = tn_dot(three_parts(rows_here), selector(3 * levels))
        second[0, body, :] = depth / (depth + speed)

    @pl.when(level == 0)
    def _():
        for y in range(0, ny, chunk):
            now = moved(first, slot, y) * second[0, pl.ds(PAD + y, chunk), :]
            out[0, 0, pl.ds(y, chunk), :] = now
            rounded[pl.ds(y, chunk), :] = now.astype(jnp.bfloat16)

    @pl.when(level != 0)
    def _():
        for y in range(0, ny, chunk):
            now = moved(first, slot, y)
            out[0, 0, pl.ds(y, chunk), :] = now
            rounded[pl.ds(y, chunk), :] = now.astype(jnp.bfloat16)

    projected = lax.dot_general(
        table[...], rounded[...], (((1,), (1,)), ((), ())), preferred_element_type=jnp.float32
    )
    bin_row = bins[pl.ds(column, 1), :]
    half = NBIN * 2 * NW
    dry = jnp.zeros((2 * NW, ny), jnp.float32)
    wet = jnp.zeros((2 * NW, ny), jnp.float32)
    for k in range(NBIN):
        chosen = bin_row == k
        dry = dry + jnp.where(chosen, projected[2 * NW * k : 2 * NW * (k + 1)], 0.0)
        wet = wet + jnp.where(chosen, projected[half + 2 * NW * k : half + 2 * NW * (k + 1)], 0.0)
    moisture = strip[column + SUB, pl.ds(2 * levels + level, 1), :]
    thickness = strip[column + SUB, pl.ds(3 * levels + level, 1), :]
    growth = moisture / (1.0 - moisture)
    opt[0, 0] = (dry + growth * wet) * thickness


def chem_call(edge, extras, shared, earlier):
    tracer, strip, bins, kinds, table, settle = shared
    levels, width, ny, species = tracer.shape
    local = 2 * SUB + 1 if edge else width
    steps = 2 * SUB if edge else width - 2 * SUB
    last = levels - 1

    if edge:
        def place(l, i):
            return (last - l, jnp.where(i < SUB, i, i + width - 2 * SUB), 0, 0)
    else:
        def place(l, i):
            return (last - l, i + SUB, 0, 0)

    def whole(l, i):
        return (last - l, 0, 0, 0)

    halo_spec = pl.BlockSpec((1, SUB, ny, species), whole)
    kept_spec = pl.BlockSpec((1, 8, ny, species), whole)
    in_specs = [pl.BlockSpec((1, width, ny, species), whole)] + [VMEM_SPEC] * 5
    inputs = (tracer,)
    aliases = {}
    if edge:
        far = width // 2 - 1
        in_specs = [SMEM_SPEC, VMEM_SPEC, halo_spec, halo_spec, kept_spec]
        in_specs += [
            pl.BlockSpec((1, 2, ny, species), whole),
            pl.BlockSpec((1, 2, ny, species), lambda l, i: (last - l, far, 0, 0)),
        ]
        in_specs += [VMEM_SPEC] * 5
        inputs = (tracer, tracer)
        in_specs += [pl.BlockSpec(memory_space=pl.ANY)] * 2
        aliases = {len(in_specs) - 2: 0, len(in_specs) - 1: 1}
    cells = levels * local * ny * species
    return pl.pallas_call(
        functools.partial(chem_kernel, levels, width, edge),
        grid=(levels, steps),
        in_specs=in_specs,
        out_specs=[
            pl.BlockSpec((1, 1, ny, species), place),
            pl.BlockSpec((1, 1, 2 * NW, ny), place),
        ]
        + ([] if edge else [kept_spec]),
        out_shape=[
            jax.ShapeDtypeStruct((levels, width, ny, species), jnp.float32),
            jax.ShapeDtypeStruct((levels, width, 2 * NW, ny), jnp.float32),
        ]
        + ([] if edge else [jax.ShapeDtypeStruct((levels, 8, ny, species), jnp.float32)]),
        scratch_shapes=[
            pltpu.VMEM((local, ny + 2 * PAD, species), jnp.float32),
            pltpu.VMEM((local, ny + 2 * PAD, species), jnp.float32),
            pltpu.VMEM((local, ny, species), jnp.float32),
            pltpu.VMEM((local, ny, species), jnp.float32),
            pltpu.VMEM((ny, species), jnp.bfloat16),
        ],
        input_output_aliases=aliases,
        compiler_params=pltpu.CompilerParams(
            dimension_semantics=("arbitrary", "arbitrary"),
            vmem_limit_bytes=60 * 1024 * 1024,
        ),
        cost_estimate=pl.CostEstimate(
            flops=cells * 40, bytes_accessed=cells * 6, transcendentals=0
        ),
        name="edge_columns" if edge else "inner_columns",
    )(*extras, *inputs, strip, bins, kinds, table, settle, *earlier)


def per_device(
    tracer_amounts,
    zonal_transit_ratio,
    meridional_transit_ratio,
    moisture_ratio,
    stratum_depths,
    sun_elevation_factor,
    thermal_anomaly,
    particle_class_map,
    ground_cover_kind,
    arid_extinction_table,
    swelling_factors,
    settling_velocities,
    arriving_irradiance,
):
    levels, width, ny, species = tracer_amounts.shape
    gx_count = lax.axis_size("gx")
    gy_count = lax.axis_size("gy")
    total = gx_count * gy_count
    gx = lax.axis_index("gx")
    gy = lax.axis_index("gy")
    tile_x, tile_y = sun_elevation_factor.shape
    both = ("gx", "gy")
    field_count = 4 * levels
    t = thermal_anomaly
    span_y = max(tile_x, tile_y)

    def edge_rows(rows):
        return jnp.pad(rows, ((0, 8 - levels), (0, span_y - rows.shape[1])))

    fringe = jnp.stack(
        [edge_rows(t[:, 0]), edge_rows(t[:, -1]), edge_rows(t[:, :, 0]), edge_rows(t[:, :, -1])]
    )
    dma = pltpu.SemaphoreType.DMA
    strip, rim, strip_sun, fringe_in = pl.pallas_call(
        functools.partial(fields_kernel, gx_count, gy_count, width),
        in_specs=[VMEM_SPEC] * 6,
        out_specs=[VMEM_SPEC] * 4,
        out_shape=[
            jax.ShapeDtypeStruct((width + 2 * SUB, field_count, ny), jnp.float32),
            jax.ShapeDtypeStruct((2, SUB, field_count, ny), jnp.float32),
            jax.ShapeDtypeStruct((width, ny), jnp.float32),
            jax.ShapeDtypeStruct(fringe.shape, jnp.float32),
        ],
        scratch_shapes=[
            pltpu.VMEM((tile_x + 2 * SUB, field_count, tile_y), jnp.float32),
            pltpu.VMEM((gy_count, width + 2 * SUB, field_count, tile_y), jnp.float32),
            dma((gy_count,)), dma((gy_count,)), dma((gy_count,)), dma((gy_count,)),
            dma((2,)), dma((gy_count,)), dma((4,)), dma((4,)),
        ],
        compiler_params=pltpu.CompilerParams(collective_id=0, has_side_effects=True),
        name="field_exchange",
    )(
        zonal_transit_ratio, meridional_transit_ratio, moisture_ratio, stratum_depths,
        sun_elevation_factor, fringe,
    )

    tail, head, strip = lax.optimization_barrier(
        (tracer_amounts[:, width - SUB :], tracer_amounts[:, :SUB], strip)
    )
    halo_w = lax.ppermute(tail, both, [(i, i + 1) for i in range(total - 1)])
    halo_e = lax.ppermute(head, both, [(i + 1, i) for i in range(total - 1)])

    east_row = jnp.where(gx == gx_count - 1, 0.0, fringe_in[0, :levels, :tile_y])
    west_row = jnp.where(gx == 0, 0.0, fringe_in[1, :levels, :tile_y])
    north_col = jnp.where(gy == gy_count - 1, 0.0, fringe_in[2, :levels, :tile_x])
    south_col = jnp.where(gy == 0, 0.0, fringe_in[3, :levels, :tile_x])
    wide_x = jnp.concatenate([west_row[:, None], t, east_row[:, None]], axis=1)
    wide_y = jnp.concatenate([south_col[:, :, None], t, north_col[:, :, None]], axis=2)
    laplace = wide_x[:, 2:] + wide_x[:, :-2] + wide_y[:, :, 2:] + wide_y[:, :, :-2] - 4.0 * t
    base = t + SPREAD_FACTOR * laplace

    table = jnp.concatenate([arid_extinction_table, swelling_factors], axis=1).T
    land = jnp.pad(
        settling_velocities, ((0, LAND_ROWS - settling_velocities.shape[0]), (0, 0))
    )
    high = lax.reduce_precision(land, 8, 7)
    middle = lax.reduce_precision(land - high, 8, 7)
    settle = jnp.concatenate([high, middle, land - high - middle], axis=0).astype(jnp.bfloat16)
    shared = (
        tracer_amounts, strip, particle_class_map, ground_cover_kind, table, settle,
    )
    updated, optical, saved = chem_call(False, (), shared, ())
    flags = jnp.stack(
        [gy == 0, (gx > 0) | (gy > 0), gy == gy_count - 1, (gx < gx_count - 1) | (gy < gy_count - 1)]
    ).astype(jnp.int32)
    updated, optical = chem_call(
        True, (flags, rim, halo_w, halo_e, saved), shared, (updated, optical)
    )
    anomaly = pl.pallas_call(
        functools.partial(return_kernel, gx_count, gy_count, width),
        in_specs=[VMEM_SPEC, VMEM_SPEC, SMEM_SPEC, VMEM_SPEC],
        out_specs=VMEM_SPEC,
        out_shape=jax.ShapeDtypeStruct(t.shape, jnp.float32),
        scratch_shapes=[
            pltpu.VMEM((gy_count, width, levels, tile_y), jnp.float32),
            pltpu.VMEM((tile_x, levels, tile_y), jnp.float32),
            dma((gy_count,)), dma((gy_count,)),
        ],
        compiler_params=pltpu.CompilerParams(collective_id=1, has_side_effects=True),
        name="heat_return",
    )(optical, strip_sun, arriving_irradiance, base)
    return (updated, anomaly)


def solution(mesh):
    return jax.shard_map(
        per_device,
        mesh=mesh,
        in_specs=(
            P(None, ("gx", "gy"), None, None),
            P(None, "gx", "gy"),
            P(None, "gx", "gy"),
            P(None, "gx", "gy"),
            P(None, "gx", "gy"),
            P("gx", "gy"),
            P(None, "gx", "gy"),
            P(("gx", "gy"), None),
            P(("gx", "gy"), None),
            P(),
            P(),
            P(),
            P(),
        ),
        out_specs=(P(None, ("gx", "gy"), None, None), P(None, "gx", "gy")),
        check_vma=False,
    )
```
